512 devices in a mesh: dp: 64 (over x, z_hi, y, core), tensor: 8 (over z_lo).
Axes of the slice: x: 4, y: 4, z: 16 (z_hi: 2, z_lo: 8; z = z_hi * 8 + z_lo), core: 2. Of those that a mesh axis runs over, the one named last changes fastest.
Arguments:
- acts: bfloat16 [8192, 2048], P('dp', 'tensor'), may hold values from -54 to 54
- partner: bfloat16 [8192, 2048], P('dp', 'tensor'), may hold values from -54 to 54
- hidden: bfloat16 [14336, 8192], P('dp', 'tensor'), may hold values from -6 to 6
- down_weight: bfloat16 [14336, 2048], P('dp', 'tensor'), may hold values from -0.046875 to 0.046875
Outputs:
- grad_hidden: bfloat16 [14336, 8192], P('dp', 'tensor')
- grad_weight: float32 [14336, 2048], P('dp', 'tensor')
- cka: float32 [], replicated
The draws below stay inside these ranges and needn't reach their ends.
All inputs are finite; a program needn't handle non-finite values.
Results may differ from the reference program's by a relative error of at most 0.0059.
Values may be sent and summed in bfloat16 or wider, within the bound.
No kernel may reach another device: no remote copies, remote signals or barrier semaphores. Data moves between devices by JAX's collectives and lax.ppermute only.
A program may use at most 64 MiB of HBM per device.

```python
import jax
import jax.numpy as jnp
from jax import lax

D = 2048
DY = 2048
FF = 14336
TOK = 128
TOKENS = 8192
LOSS_SCALE = 16777216
N_DP = 64


def feature_draw(key, rows, cols):
    key_row, key_col, key_mean, key_base = jax.random.split(key, 4)
    place = jnp.arange(rows, dtype=jnp.float32) / rows
    base = jnp.clip(jax.random.normal(key_base, (rows, cols), jnp.float32), -3.5, 3.5)
    trend = 0.8 + 0.6 * place
    row_scale = trend[:, None] * jnp.exp(jax.random.uniform(key_row, (rows, 1), jnp.float32, -1.15, 1.15))
    col_scale = jnp.exp(jax.random.uniform(key_col, (1, cols), jnp.float32, -1.15, 1.15))
    col_mean = 0.5 * jnp.clip(jax.random.normal(key_mean, (1, cols), jnp.float32), -3.0, 3.0)
    return (base * row_scale + col_mean) * col_scale


def draw_acts(key, part):
    return feature_draw(jax.random.fold_in(key, 11), TOKENS, D).astype(jnp.bfloat16)


def draw_partner(key, part):
    return feature_draw(jax.random.fold_in(key, 23), TOKENS, DY).astype(jnp.bfloat16)


def block_levels(stream_key, extent, cuts, low, largest):
    loudness, own = 1.0, jax.random.fold_in(stream_key, 6)
    for dim, parts in cuts:
        steps = jnp.exp(jax.random.uniform(jax.random.fold_in(own, dim), (parts,), jnp.float32, low / len(cuts), largest / len(cuts)))
        loudness = loudness * jnp.repeat(steps, extent[dim] // parts).reshape([-1 if axis == dim else 1 for axis in range(len(extent))])
    return loudness


def scatter_about(rng, dims, deviation, bound, pieces=(), kind=jnp.bfloat16):
    gain = block_levels(rng, dims, pieces, -0.22, 0.18) if pieces else 1.0
    entries = jax.random.normal(rng, dims, jnp.float32) * deviation * gain
    return jnp.minimum(jnp.maximum(entries, -bound), bound).astype(kind)


def setup_inputs(seed: int = 0) -> dict:
    seeds = jax.random.split(jax.random.key(seed), 5)
    return {
        "acts": draw_acts(jax.random.fold_in(seeds[4], 71), 0),
        "partner": draw_partner(jax.random.fold_in(seeds[4], 71), 0),
        "hidden": scatter_about(seeds[2], (FF, TOKENS), 1.0, 6.0, ((0, 64), (1, 8))),
        "down_weight": scatter_about(seeds[3], (FF, D), FF ** -0.5, 0.046875, ((0, 64), (1, 8))),
    }


def center(values, width):
    blocks = values.astype(jnp.float32).reshape(N_DP, TOK, width)
    return (blocks - lax.optimization_barrier(jnp.mean(blocks, axis=1, keepdims=True))).astype(jnp.bfloat16)

def reference(acts, partner, hidden, down_weight):
    xc = center(acts, D)
    yc = center(partner, DY)
    xf = xc.astype(jnp.float32)
    yf = yc.astype(jnp.float32)
    gram_x = jnp.einsum('bnd,bmd->bnm', xf, xf)
    gram_y = jnp.einsum('bnd,bmd->bnm', yf, yf)
    sxx = jnp.sum(gram_x * gram_x)
    syy = jnp.sum(gram_y * gram_y)
    sxy = jnp.sum(gram_x * gram_y)
    root = jnp.sqrt(sxx * syy)
    cka = sxy / root
    ratio = sxy / sxx
    coef = -2.0 * jnp.float32(LOSS_SCALE) / root
    mixed = gram_y - ratio * gram_x
    grad = coef * jnp.einsum('bnm,bmd->bnd', mixed, xf, precision=lax.Precision.HIGHEST)
    grad = grad.astype(jnp.bfloat16).reshape(TOKENS, D)
    grad_hidden = jnp.dot(down_weight, grad.T, preferred_element_type=jnp.float32).astype(jnp.bfloat16)
    grad_weight = jnp.dot(hidden, grad, preferred_element_type=jnp.float32)
    return (grad_hidden, grad_weight, cka)
```

```python
import itertools

import jax
import jax.numpy as jnp
from jax import lax
from jax.sharding import Mesh, PartitionSpec as P

NAMES = ("x", "zh", "y", "c", "t")
SIZES = {"x": 4, "zh": 2, "y": 4, "c": 2, "t": 8}
BF16 = jnp.bfloat16
F32 = jnp.float32


def center_rows(values):
    floats = values.astype(F32)
    return (floats - jnp.mean(floats, axis=0, keepdims=True)).astype(BF16)


def permutation(names, target):
    pairs = []
    for place in itertools.product(*[range(SIZES[n]) for n in names]):
        goal = target(dict(zip(names, place)))
        source, dest = 0, 0
        for name, coordinate in zip(names, place):
            source = source * SIZES[name] + coordinate
            dest = dest * SIZES[name] + goal[name]
        pairs.append((source, dest))
    return pairs


def permute(values, names, target):
    return lax.ppermute(values, names, permutation(names, target))


def to_plane(flip):
    def target(d):
        return {"x": d["t"] // 2, "zh": (d["t"] + flip) % 2, "t": 2 * d["x"] + d["zh"]}

    return target


def gather_weight(weight):
    blocks = weight[None]
    t = lax.axis_index("t")
    for bit in (1, 2, 4):
        other = permute(blocks, ("t",), lambda d, bit=bit: {"t": d["t"] ^ bit})
        low = (t & bit) == 0
        blocks = jnp.concatenate(
            [jnp.where(low, blocks, other), jnp.where(low, other, blocks)], axis=0
        )
    return blocks


def local(acts, partner, hidden, down_weight):
    rows, width = acts.shape
    units = hidden.shape[0]
    scale = float(rows * 64 * width * 8)
    both = jnp.concatenate([center_rows(acts), center_rows(partner)], axis=1)
    first = permute(both, ("x", "zh", "t"), to_plane(0))
    second = permute(both, ("x", "zh", "t"), to_plane(1))
    weights = gather_weight(down_weight)
    even = lax.axis_index("zh") == 0
    low = jnp.where(even, first, second)
    high = jnp.where(even, second, first)
    y_pair = jnp.concatenate([low[:, width:], high[:, width:]], axis=1)
    gram_y = lax.dot_general(
        y_pair, y_pair, (((1,), (1,)), ((), ())), preferred_element_type=F32
    ).astype(BF16)
    chunk = jnp.concatenate([low[:, :width], high[:, :width], gram_y], axis=1)
    chunks = jnp.broadcast_to(chunk[None], (16,) + chunk.shape)
    plane = lax.all_to_all(chunks, ("x", "y"), split_axis=0, concat_axis=0)
    other = permute(plane, ("c",), lambda d: {"c": 1 - d["c"]})
    core = lax.axis_index("c") == 0
    pair = jnp.stack([jnp.where(core, plane, other), jnp.where(core, other, plane)])
    pair = pair.reshape(2, 4, 4, rows, 2 * width + rows)
    xs = pair[..., : 2 * width].transpose(2, 0, 3, 1, 4).reshape(8, rows, 8 * width)
    grams_y = jnp.sum(pair[..., 2 * width :].astype(F32), axis=1)
    grams_y = grams_y.transpose(1, 0, 2, 3).reshape(8, rows, rows)
    grams_x = lax.dot_general(
        xs, xs, (((2,), (2,)), ((0,), (0,))), preferred_element_type=F32
    )
    sums = jnp.stack(
        [jnp.sum(grams_x * grams_x), jnp.sum(grams_y * grams_y), jnp.sum(grams_x * grams_y)]
    )
    tile = jnp.broadcast_to(sums[None, :, None], (8, 3, 128))
    tiles = lax.all_to_all(tile, ("t",), split_axis=0, concat_axis=0)
    sums = jnp.sum(tiles, axis=0)[:, 0]
    sxx, syy, sxy = sums[0], sums[1], sums[2]
    root = jnp.sqrt(sxx * syy)
    cka = sxy / root
    ratio = sxy / sxx
    coef = -2.0 * scale / root
    mixed = grams_y - ratio * grams_x
    mixed_high = mixed.astype(BF16)
    mixed_low = (mixed - mixed_high.astype(F32)).astype(BF16)
    product = lax.dot_general(
        jnp.concatenate([mixed_high, mixed_low], axis=1),
        xs,
        (((2,), (1,)), ((0,), (0,))),
        preferred_element_type=F32,
    )
    grad = (coef * (product[:, :rows] + product[:, rows:])).astype(BF16)
    grad = grad.reshape(8 * rows, 8 * width)
    partial = lax.dot_general(
        hidden, grad, (((1,), (0,)), ((), ())), preferred_element_type=F32
    ).astype(BF16)
    parts = partial.reshape(units, 8, width).transpose(1, 0, 2)
    parts = lax.all_to_all(parts, ("t",), split_axis=0, concat_axis=0)
    grad_weight = jnp.sum(parts.astype(F32), axis=0)
    full_weight = weights.transpose(1, 0, 2).reshape(units, 8 * width)
    grad_hidden = lax.dot_general(
        full_weight, grad, (((1,), (1,)), ((), ())), preferred_element_type=F32
    ).astype(BF16)
    return (grad_hidden, grad_weight, cka)


def solution(mesh):
    shape = tuple(SIZES[n] for n in NAMES)
    fine = Mesh(mesh.devices.reshape(shape), NAMES)
    spec = P(("x", "zh", "y", "c"), "t")
    return jax.shard_map(
        local, mesh=fine, in_specs=(spec,) * 4, out_specs=(spec, spec, P()), check_vma=False
    )
```

```python
import functools
import itertools

import jax
import jax.numpy as jnp
from jax import lax
from jax.experimental import pallas as pl
from jax.experimental.pallas import tpu as pltpu
from jax.sharding import Mesh, PartitionSpec as P


NAMES = ("x", "zh", "y", "c", "t")
SIZES = {"x": 4, "zh": 2, "y": 4, "c": 2, "t": 8}
BF16 = jnp.bfloat16
F32 = jnp.float32
ROWS = 128
WIDTH = 256
SLICE = ROWS // 8
PIECE = ROWS + SLICE
CHUNK = 2 * PIECE + 16


def permutation(names, target):
    pairs = []
    for place in itertools.product(*[range(SIZES[n]) for n in names]):
        goal = target(dict(zip(names, place)))
        source, dest = 0, 0
        for name, coordinate in zip(names, place):
            source = source * SIZES[name] + coordinate
            dest = dest * SIZES[name] + goal[name]
        pairs.append((source, dest))
    return pairs


def permute(values, names, target):
    return lax.ppermute(values, names, permutation(names, target))


def exchange(values, names):
    return lax.all_to_all(values, names, split_axis=0, concat_axis=0)


def to_plane(flip):
    def target(d):
        return {"x": d["t"] // 2, "zh": (d["t"] + flip) % 2, "t": 2 * d["x"] + d["zh"]}

    return target


def gram(values):
    return lax.dot_general(values, values, (((1,), (1,)), ((), ())), preferred_element_type=F32)


def center(values):
    floats = values.astype(F32)
    return (floats - jnp.mean(floats, axis=0, keepdims=True)).astype(BF16)


def source_kernel(acts_ref, partner_ref, x_ref, grams_ref):
    x = center(acts_ref[...])
    x_ref[...] = x
    y = center(partner_ref[...])
    grams_ref[:, :SLICE, :] = gram(x).reshape(8, SLICE, ROWS)
    grams_ref[:, SLICE:, :] = gram(y).reshape(8, SLICE, ROWS)


def split(values, parts):
    pieces = []
    for _ in range(parts):
        piece = values.astype(BF16)
        values = values - piece.astype(F32)
        pieces.append(piece)
    return pieces


def slice_kernel(x_ref, parts_ref, piece_ref, tiles_ref):
    total = jnp.sum(parts_ref[...], axis=0)
    gx, gy = total[:SLICE], total[SLICE:]
    piece_ref[:ROWS, :] = x_ref[...]
    high, low = split(gy, 2)
    piece_ref[ROWS:, :ROWS] = high
    piece_ref[ROWS:, ROWS:] = low
    rows = [jnp.sum(v, axis=0, keepdims=True) for v in (gx * gx, gy * gy, gx * gy)]
    tile = jnp.concatenate(rows + [jnp.zeros((5, ROWS), F32)], axis=0)
    tiles_ref[...] = jnp.broadcast_to(tile[None], tiles_ref.shape)


def chunk_kernel(flag_ref, first_ref, second_ref, tiles_ref, chunk_ref):
    even = flag_ref[0] == 0
    first, second = first_ref[...], second_ref[...]
    low = jnp.where(even, first, second)
    high = jnp.where(even, second, first)
    chunk_ref[:ROWS, :] = low[:ROWS]
    chunk_ref[ROWS : 2 * ROWS, :] = high[:ROWS]
    chunk_ref[2 * ROWS : 2 * ROWS + SLICE, :] = low[ROWS:]
    chunk_ref[2 * ROWS + SLICE : 2 * PIECE, :] = high[ROWS:]
    total = jnp.sum(tiles_ref[...], axis=0)[:3]
    pieces = [p.astype(F32) for p in split(total, 3)]
    block = jnp.concatenate(pieces + [jnp.zeros((7, ROWS), F32)], axis=0)
    chunk_ref[2 * PIECE :, :] = jnp.concatenate([block, block], axis=1).astype(BF16)


def main_kernel(
    scale, core_ref, own_ref, other_ref, own_sums_ref, other_sums_ref, hidden_ref,
    grad_ref, parts_ref, cka_ref, sums_ref, total_ref,
):
    step = pl.program_id(0)

    @pl.when(step == 0)
    def _():
        tiles = own_sums_ref[...].astype(F32) + other_sums_ref[...].astype(F32)
        block = jnp.sum(tiles.reshape(16, 16, WIDTH), axis=0)[:, :ROWS]
        sums = block[0:3] + block[3:6] + block[6:9]
        sums = jnp.sum(sums, axis=1, keepdims=True)
        sxx, syy, sxy = sums[0:1], sums[1:2], sums[2:3]
        root = jnp.sqrt(sxx * syy)
        sums_ref[0:1, :] = jnp.broadcast_to(sxy / sxx, (1, ROWS))
        sums_ref[1:2, :] = jnp.broadcast_to(-2.0 * scale / root, (1, ROWS))
        cka_ref[...] = jnp.broadcast_to(sxy / root, cka_ref.shape)

    def work(block_ref):
        pieces = [block_ref[t // 2, 0, pl.ds((t % 2) * ROWS, ROWS), :] for t in range(8)]
        gx = gram(pieces[0])
        for piece in pieces[1:]:
            gx = gx + gram(piece)
        slices = []
        for t in range(8):
            rows = block_ref[t // 2, 0, pl.ds(2 * ROWS + (t % 2) * SLICE, SLICE), :].astype(F32)
            slices.append(rows[:, :ROWS] + rows[:, ROWS:])
        gy = jnp.concatenate(slices, axis=0)
        mixed = gy - sums_ref[0:1, :] * gx
        high, low = split(mixed, 2)
        both = jnp.concatenate([high, low], axis=0)
        coef = sums_ref[1:2, :]
        coef = jnp.concatenate([coef, coef], axis=1)
        for t in range(8):
            product = jnp.dot(both, pieces[t], preferred_element_type=F32)
            block = (coef * (product[:ROWS] + product[ROWS:])).astype(BF16)
            columns = slice(t * WIDTH, (t + 1) * WIDTH)
            grad_ref[:, columns] = block
            added = jnp.dot(hidden_ref[...], block, preferred_element_type=F32)

            @pl.when(step == 0)
            def _():
                total_ref[:, columns] = added

            @pl.when(jnp.logical_and(step > 0, step < 7))
            def _():
                total_ref[:, columns] += added

            @pl.when(step == 7)
            def _():
                parts_ref[t] = (total_ref[:, columns] + added).astype(BF16)

    @pl.when(step < 4)
    def _():
        work(own_ref)

    @pl.when(step >= 4)
    def _():
        work(other_ref)


def combine(core, plane, other, hidden, scale):
    units = hidden.shape[0]
    plane = plane.reshape(4, 4, CHUNK, WIDTH)
    other = other.reshape(4, 4, CHUNK, WIDTH)

    def place(i, core):
        return lax.rem(i, 4) * 2 + lax.rem(core[0] + i // 4, 2)

    sums = pl.BlockSpec((4, 4, 16, WIDTH), lambda i, core: (0, 0, 2 * PIECE // 16, 0))
    return pl.pallas_call(
        functools.partial(main_kernel, scale),
        grid_spec=pltpu.PrefetchScalarGridSpec(
            num_scalar_prefetch=1,
            grid=(8,),
            in_specs=[
                pl.BlockSpec((4, 1, CHUNK, WIDTH), lambda i, core: (0, jnp.minimum(i, 3), 0, 0)),
                pl.BlockSpec((4, 1, CHUNK, WIDTH), lambda i, core: (0, jnp.maximum(i - 4, 0), 0, 0)),
                sums,
                sums,
                pl.BlockSpec((units, ROWS), lambda i, core: (0, place(i, core))),
            ],
            out_specs=[
                pl.BlockSpec((ROWS, 8 * WIDTH), lambda i, core: (place(i, core), 0)),
                pl.BlockSpec((8, units, WIDTH), lambda i, core: (0, 0, 0)),
                pl.BlockSpec((8, ROWS), lambda i, core: (0, 0)),
            ],
            scratch_shapes=[pltpu.VMEM((8, ROWS), F32), pltpu.VMEM((units, 8 * WIDTH), F32)],
        ),
        out_shape=[
            jax.ShapeDtypeStruct((8 * ROWS, 8 * WIDTH), BF16),
            jax.ShapeDtypeStruct((8, units, WIDTH), BF16),
            jax.ShapeDtypeStruct((8, ROWS), F32),
        ],
        compiler_params=pltpu.CompilerParams(vmem_limit_bytes=32 << 20),
        name="combine",
    )(core, plane, other, plane, other, hidden)


def hidden_kernel(place_ref, near_ref, far_ref, grad_ref, out_ref, total_ref):
    step = pl.program_id(0)

    def add(weight):
        product = lax.dot_general(
            weight, grad_ref[...], (((1,), (1,)), ((), ())), preferred_element_type=F32
        )

        @pl.when(step == 0)
        def _():
            total_ref[...] = product

        @pl.when(jnp.logical_and(step > 0, step < 7))
        def _():
            total_ref[...] += product

        @pl.when(step == 7)
        def _():
            out_ref[...] = (total_ref[...] + product).astype(BF16)

    @pl.when(step < 4)
    def _():
        add(near_ref[0])

    @pl.when(step >= 4)
    def _():
        add(far_ref[0])


def hidden_gradient(place, near, far, grad):
    units = near.shape[1]

    def column(k, place):
        bits = lax.rem(k, 2) * 4 + lax.rem(k // 2, 2) * 2 + k // 4
        return lax.bitwise_xor(place[0], bits)

    tokens = grad.shape[0]
    return pl.pallas_call(
        hidden_kernel,
        grid_spec=pltpu.PrefetchScalarGridSpec(
            num_scalar_prefetch=1,
            grid=(8,),
            in_specs=[
                pl.BlockSpec((1, units, WIDTH), lambda k, place: (jnp.minimum(k, 3), 0, 0)),
                pl.BlockSpec((1, units, WIDTH), lambda k, place: (jnp.maximum(k - 4, 0), 0, 0)),
                pl.BlockSpec((tokens, WIDTH), lambda k, place: (0, column(k, place))),
            ],
            out_specs=pl.BlockSpec((units, tokens), lambda k, place: (0, 0)),
            scratch_shapes=[pltpu.VMEM((units, tokens), F32)],
        ),
        out_shape=jax.ShapeDtypeStruct((units, tokens), BF16),
        cost_estimate=pl.CostEstimate(
            flops=2 * units * tokens * 8 * WIDTH, bytes_accessed=6 << 20, transcendentals=0
        ),
        name="hidden_gradient",
    )(place, near, far, grad)


def local(acts, partner, hidden, down_weight):
    scale = float(ROWS * 64 * WIDTH * 8)
    vmem = pl.BlockSpec(memory_space=pltpu.VMEM)
    smem = pl.BlockSpec(memory_space=pltpu.SMEM)
    shape = jax.ShapeDtypeStruct
    near = down_weight[None]
    far = permute(near, ("t",), lambda d: {"t": d["t"] ^ 4})
    near = jnp.concatenate([near, far], axis=0)
    far = permute(near, ("t",), lambda d: {"t": d["t"] ^ 2})
    near = jnp.concatenate([near, far], axis=0)
    far = permute(near, ("t",), lambda d: {"t": d["t"] ^ 1})
    x, grams = pl.pallas_call(
        source_kernel,
        in_specs=[vmem, vmem],
        out_specs=[vmem, vmem],
        out_shape=[shape((ROWS, WIDTH), BF16), shape((8, 2 * SLICE, ROWS), F32)],
        name="source",
    )(acts, partner)
    grams = exchange(grams, ("t",))
    piece, tiles = pl.pallas_call(
        slice_kernel,
        in_specs=[vmem, vmem],
        out_specs=[vmem, vmem],
        out_shape=[shape((PIECE, WIDTH), BF16), shape((16, 8, ROWS), F32)],
        name="slices",
    )(x, grams)
    first = permute(piece, ("x", "zh", "t"), to_plane(0))
    second = permute(piece, ("x", "zh", "t"), to_plane(1))
    tiles = exchange(tiles, ("zh", "t"))
    flag = lax.axis_index("zh").astype(jnp.int32).reshape(1)
    chunk = pl.pallas_call(
        chunk_kernel,
        in_specs=[smem, vmem, vmem, vmem],
        out_specs=vmem,
        out_shape=shape((CHUNK, WIDTH), BF16),
        name="chunk",
    )(flag, first, second, tiles)
    plane = exchange(jnp.broadcast_to(chunk[None], (16,) + chunk.shape), ("x", "y"))
    other = permute(plane, ("c",), lambda d: {"c": 1 - d["c"]})
    core = lax.axis_index("c").astype(jnp.int32).reshape(1)
    grad, parts, cka = combine(core, plane, other, hidden, scale)
    parts = exchange(parts, ("t",))
    grad_weight = jnp.sum(parts.astype(F32), axis=0)
    place = lax.axis_index("t").astype(jnp.int32).reshape(1)
    grad_hidden = hidden_gradient(place, near, far, grad)
    return (grad_hidden, grad_weight, cka[0, 0])


def solution(mesh):
    shape = tuple(SIZES[n] for n in NAMES)
    fine = Mesh(mesh.devices.reshape(shape), NAMES)
    spec = P(("x", "zh", "y", "c"), "t")
    return jax.shard_map(
        local, mesh=fine, in_specs=(spec,) * 4, out_specs=(spec, spec, P()), check_vma=False
    )
```

```python
import functools
import itertools

import jax
import jax.numpy as jnp
from jax import lax
from jax.experimental import pallas as pl
from jax.experimental.pallas import tpu as pltpu
from jax.sharding import Mesh, PartitionSpec as P


NAMES = ("x", "zh", "y", "c", "t")
SIZES = {"x": 4, "zh": 2, "y": 4, "c": 2, "t": 8}
BF16 = jnp.bfloat16
F32 = jnp.float32
ROWS = 128
WIDTH = 256
SLICE = ROWS // 8
PIECE = ROWS + SLICE
CHUNK = 2 * PIECE + 16


def permutation(names, target):
    pairs = []
    for place in itertools.product(*[range(SIZES[n]) for n in names]):
        goal = target(dict(zip(names, place)))
        source, dest = 0, 0
        for name, coordinate in zip(names, place):
            source = source * SIZES[name] + coordinate
            dest = dest * SIZES[name] + goal[name]
        pairs.append((source, dest))
    return pairs


def permute(values, names, target):
    return lax.ppermute(values, names, permutation(names, target))


def exchange(values, names):
    return lax.all_to_all(values, names, split_axis=0, concat_axis=0)


def to_plane(flip):
    def target(d):
        return {"x": d["t"] // 2, "zh": (d["t"] + flip) % 2, "t": 2 * d["x"] + d["zh"]}

    return target


def gram(values):
    return lax.dot_general(values, values, (((1,), (1,)), ((), ())), preferred_element_type=F32)


def center(values):
    floats = values.astype(F32)
    return (floats - jnp.mean(floats, axis=0, keepdims=True)).astype(BF16)


def source_kernel(acts_ref, partner_ref, x_ref, grams_ref):
    x = center(acts_ref[...])
    x_ref[...] = x
    y = center(partner_ref[...])
    grams_ref[:, :SLICE, :] = gram(x).reshape(8, SLICE, ROWS)
    grams_ref[:, SLICE:, :] = gram(y).reshape(8, SLICE, ROWS)


def split(values, parts):
    pieces = []
    for _ in range(parts):
        piece = values.astype(BF16)
        values = values - piece.astype(F32)
        pieces.append(piece)
    return pieces


def slice_kernel(x_ref, parts_ref, piece_ref, sums_ref):
    total = jnp.sum(parts_ref[...], axis=0)
    gx, gy = total[:SLICE], total[SLICE:]
    piece_ref[:ROWS, :] = x_ref[...]
    high, low = split(gy, 2)
    piece_ref[ROWS:, :ROWS] = high
    piece_ref[ROWS:, ROWS:] = low
    rows = [jnp.sum(v, axis=0, keepdims=True) for v in (gx * gx, gy * gy, gx * gy)]
    rows = [p.astype(F32) for p in split(jnp.concatenate(rows, axis=0), 3)]
    block = jnp.concatenate(rows + [jnp.zeros((7, ROWS), F32)], axis=0)
    sums_ref[...] = jnp.concatenate([block, jnp.zeros_like(block)], axis=1).astype(BF16)


def sums_kernel(rows_ref, tiles_ref):
    block = jnp.sum(rows_ref[...].astype(F32).reshape(16, 16, WIDTH), axis=0)[:, :ROWS]
    sums = block[0:3] + block[3:6] + block[6:9]
    tile = jnp.concatenate([sums, jnp.zeros((5, ROWS), F32)], axis=0)
    tiles_ref[...] = jnp.broadcast_to(tile[None], tiles_ref.shape)


def plane_sums(plane):
    return pl.pallas_call(
        sums_kernel,
        grid=(1,),
        in_specs=[pl.BlockSpec((4, 4, 16, WIDTH), lambda i: (0, 0, 2 * PIECE // 16, 0))],
        out_specs=pl.BlockSpec((32, 8, ROWS), lambda i: (0, 0, 0)),
        out_shape=jax.ShapeDtypeStruct((32, 8, ROWS), F32),
        name="plane_sums",
    )(plane)


def gram_kernel(block_ref, out_ref):
    pieces = [block_ref[t // 2, 0, pl.ds((t % 2) * ROWS, ROWS), :] for t in range(8)]
    out_ref[0] = gram(jnp.concatenate(pieces, axis=1))


def plane_grams(plane):
    return pl.pallas_call(
        gram_kernel,
        grid=(4,),
        in_specs=[pl.BlockSpec((4, 1, CHUNK, WIDTH), lambda i: (0, i, 0, 0))],
        out_specs=pl.BlockSpec((1, ROWS, ROWS), lambda i: (i, 0, 0)),
        out_shape=jax.ShapeDtypeStruct((4, ROWS, ROWS), F32),
        cost_estimate=pl.CostEstimate(
            flops=4 << 30, bytes_accessed=16 << 20, transcendentals=0
        ),
        name="plane_grams",
    )(plane)


def mix_kernel(
    scale, core_ref, own_gram_ref, other_gram_ref, own_rows_ref, other_rows_ref, tiles_ref,
    hidden_ref, mixed_ref, product_ref, cka_ref,
):
    sums = jnp.sum(jnp.sum(tiles_ref[...], axis=0), axis=1, keepdims=True)
    sxx, syy, sxy = sums[0:1], sums[1:2], sums[2:3]
    root = jnp.sqrt(sxx * syy)
    ratio = jnp.broadcast_to(sxy / sxx, (1, ROWS))
    coef = jnp.broadcast_to(-2.0 * scale / root, (1, ROWS))
    cka_ref[...] = jnp.broadcast_to(sxy / root, cka_ref.shape)
    core = core_ref[0]
    for b in range(8):
        y = b % 4
        gram_ref, rows_ref = (own_gram_ref, own_rows_ref) if b < 4 else (other_gram_ref, other_rows_ref)
        slices = []
        for t in range(8):
            rows = rows_ref[t // 2, y, pl.ds((t % 2) * SLICE, SLICE), :].astype(F32)
            slices.append(rows[:, :ROWS] + rows[:, ROWS:])
        mixed = coef * (jnp.concatenate(slices, axis=0) - ratio * gram_ref[y])
        mixed_ref[b] = mixed
        place = y * 2 + (core if b < 4 else 1 - core)
        hidden = hidden_ref[:, pl.ds(pl.multiple_of(place * ROWS, ROWS), ROWS)]
        product = jnp.dot(
            jnp.concatenate([hidden, hidden], axis=1),
            jnp.concatenate(split(mixed, 2), axis=0),
            preferred_element_type=F32,
        )
        product_ref[:, b * ROWS : (b + 1) * ROWS] = product.astype(BF16)


def mix(core, own_gram, other_gram, plane, other, tiles, hidden, scale):
    units = hidden.shape[0]
    smem = pl.BlockSpec(memory_space=pltpu.SMEM)
    rows = pl.BlockSpec((4, 4, 2 * SLICE, WIDTH), lambda i: (0, 0, ROWS // SLICE, 0))
    whole = lambda *shape: pl.BlockSpec(shape, lambda i: (0,) * len(shape))
    return pl.pallas_call(
        functools.partial(mix_kernel, scale),
        grid=(1,),
        in_specs=[
            smem,
            whole(4, ROWS, ROWS),
            whole(4, ROWS, ROWS),
            rows,
            rows,
            whole(32, 8, ROWS),
            whole(units, 8 * ROWS),
        ],
        out_specs=[whole(8, ROWS, ROWS), whole(units, 8 * ROWS), whole(8, ROWS)],
        out_shape=[
            jax.ShapeDtypeStruct((8, ROWS, ROWS), F32),
            jax.ShapeDtypeStruct((units, 8 * ROWS), BF16),
            jax.ShapeDtypeStruct((8, ROWS), F32),
        ],
        name="mix",
    )(core, own_gram, other_gram, plane, other, tiles, hidden)


def reversed_bits(k):
    return lax.rem(k, 2) * 4 + lax.rem(k // 2, 2) * 2 + k // 4


def column_blocks(first):
    def index(k, place):
        t = lax.bitwise_xor(place[0], reversed_bits(first + k))
        return (t // 2, 0, lax.rem(t, 2), 0)

    return pl.BlockSpec((1, 4, ROWS, WIDTH), index)


def weight_kernel(place_ref, product_ref, own_ref, other_ref, out_ref):
    half = 4 * ROWS
    value = jnp.dot(
        product_ref[:, :half], own_ref[...].reshape(half, WIDTH), preferred_element_type=F32
    )
    value = value + jnp.dot(
        product_ref[:, half:], other_ref[...].reshape(half, WIDTH), preferred_element_type=F32
    )
    out_ref[0] = value.astype(out_ref.dtype)


def weight_parts(place, product, plane, other, first, dtype):
    units = product.shape[0]
    return pl.pallas_call(
        weight_kernel,
        grid_spec=pltpu.PrefetchScalarGridSpec(
            num_scalar_prefetch=1,
            grid=(4,),
            in_specs=[
                pl.BlockSpec((units, 8 * ROWS), lambda k, place: (0, 0)),
                column_blocks(first),
                column_blocks(first),
            ],
            out_specs=pl.BlockSpec((1, units, WIDTH), lambda k, place: (k, 0, 0)),
        ),
        out_shape=jax.ShapeDtypeStruct((4, units, WIDTH), dtype),
        cost_estimate=pl.CostEstimate(
            flops=2 * units * 8 * ROWS * 4 * WIDTH, bytes_accessed=4 << 20, transcendentals=0
        ),
        name="weight_parts",
    )(place, product, plane, other)


def hidden_kernel(
    place_ref, core_ref, near_ref, far_ref, own_ref, other_ref, mixed_ref, out_ref, total_ref
):
    step = pl.program_id(0)
    half = 4 * ROWS
    weight = jnp.where(step < 4, near_ref[0], far_ref[0])
    for ref, columns in ((own_ref, slice(0, half)), (other_ref, slice(half, 2 * half))):
        product = lax.dot_general(
            weight,
            ref[...].reshape(half, WIDTH),
            (((1,), (1,)), ((), ())),
            preferred_element_type=F32,
        )

        @pl.when(step == 0)
        def _(product=product, columns=columns):
            total_ref[:, columns] = product

        @pl.when(step > 0)
        def _(product=product, columns=columns):
            total_ref[:, columns] += product

    @pl.when(step == 7)
    def _():
        for b in range(8):
            high, low = split(total_ref[:, b * ROWS : (b + 1) * ROWS], 2)
            mixed_high, mixed_low = split(mixed_ref[b], 2)
            value = lax.dot_general(
                jnp.concatenate([high, high, low], axis=1),
                jnp.concatenate([mixed_high, mixed_low, mixed_high], axis=1),
                (((1,), (1,)), ((), ())),
                preferred_element_type=F32,
            )
            place = b % 4 * 2 + (core_ref[0] if b < 4 else 1 - core_ref[0])
            out_ref[:, pl.ds(pl.multiple_of(place * ROWS, ROWS), ROWS)] = value.astype(BF16)


def hidden_gradient(place, core, near, far, plane, other, mixed):
    units = near.shape[1]
    tokens = 8 * ROWS
    blocks = pl.BlockSpec(
        (1, 4, ROWS, WIDTH), lambda k, place, core: column_blocks(0).index_map(k, place)
    )
    return pl.pallas_call(
        hidden_kernel,
        grid_spec=pltpu.PrefetchScalarGridSpec(
            num_scalar_prefetch=2,
            grid=(8,),
            in_specs=[
                pl.BlockSpec((1, units, WIDTH), lambda k, *_: (jnp.minimum(k, 3), 0, 0)),
                pl.BlockSpec((1, units, WIDTH), lambda k, *_: (jnp.maximum(k - 4, 0), 0, 0)),
                blocks,
                blocks,
                pl.BlockSpec((8, ROWS, ROWS), lambda k, *_: (0, 0, 0)),
            ],
            out_specs=pl.BlockSpec((units, tokens), lambda k, *_: (0, 0)),
            scratch_shapes=[pltpu.VMEM((units, tokens), F32)],
        ),
        out_shape=jax.ShapeDtypeStruct((units, tokens), BF16),
        cost_estimate=pl.CostEstimate(
            flops=2 * units * tokens * 8 * WIDTH, bytes_accessed=8 << 20, transcendentals=0
        ),
        name="hidden_gradient",
    )(place, core, near, far, plane, other, mixed)


def flip(bit):
    return lambda d: {"t": d["t"] ^ bit}


def local(acts, partner, hidden, down_weight):
    scale = float(ROWS * 64 * WIDTH * 8)
    vmem = pl.BlockSpec(memory_space=pltpu.VMEM)
    shape = jax.ShapeDtypeStruct
    place = lax.axis_index("t").astype(jnp.int32).reshape(1)
    core = lax.axis_index("c").astype(jnp.int32).reshape(1)
    near = down_weight[None]
    far = permute(near, ("t",), flip(4))
    near = jnp.concatenate([near, far], axis=0)
    far = permute(near, ("t",), flip(2))
    near = jnp.concatenate([near, far], axis=0)
    far = permute(near, ("t",), flip(1))
    x, grams = pl.pallas_call(
        source_kernel,
        in_specs=[vmem, vmem],
        out_specs=[vmem, vmem],
        out_shape=[shape((ROWS, WIDTH), BF16), shape((8, 2 * SLICE, ROWS), F32)],
        name="source",
    )(acts, partner)
    grams = exchange(grams, ("t",))
    piece, sums = pl.pallas_call(
        slice_kernel,
        in_specs=[vmem, vmem],
        out_specs=[vmem, vmem],
        out_shape=[shape((PIECE, WIDTH), BF16), shape((16, WIDTH), BF16)],
        name="slices",
    )(x, grams)
    first = permute(piece, ("x", "zh", "t"), to_plane(0))
    second = permute(piece, ("x", "zh", "t"), to_plane(1))
    even = lax.axis_index("zh") == 0
    low = jnp.where(even, first, second)
    high = jnp.where(even, second, first)
    chunk = jnp.concatenate([low[:ROWS], high[:ROWS], low[ROWS:], high[ROWS:], sums], axis=0)
    plane = exchange(jnp.broadcast_to(chunk[None], (16,) + chunk.shape), ("x", "y"))
    other = permute(plane, ("c",), lambda d: {"c": 1 - d["c"]})
    plane = plane.reshape(4, 4, CHUNK, WIDTH)
    other = other.reshape(4, 4, CHUNK, WIDTH)
    tiles = plane_sums(plane)
    tiles = exchange(tiles, ("zh", "c", "t"))
    mixed, product, cka = mix(
        core, plane_grams(plane), plane_grams(other), plane, other, tiles, hidden, scale
    )
    sent = weight_parts(place, product, plane, other, 4, BF16)
    sent = permute(sent, ("t",), flip(1))
    kept = weight_parts(place, product, plane, other, 0, F32)
    later = permute((kept[2:] + sent[2:].astype(F32)).astype(BF16), ("t",), flip(2))
    kept = kept[:2] + sent[:2].astype(F32)
    last = permute((kept[1] + later[1].astype(F32)).astype(BF16), ("t",), flip(4))
    grad_weight = kept[0] + later[0].astype(F32) + last.astype(F32)
    grad_hidden = hidden_gradient(place, core, near, far, plane, other, mixed)
    return (grad_hidden, grad_weight, cka[0, 0])


def solution(mesh):
    shape = tuple(SIZES[n] for n in NAMES)
    fine = Mesh(mesh.devices.reshape(shape), NAMES)
    spec = P(("x", "zh", "y", "c"), "t")
    return jax.shard_map(
        local, mesh=fine, in_specs=(spec,) * 4, out_specs=(spec, spec, P()), check_vma=False
    )
```

```python
import functools
import itertools

import jax
import jax.numpy as jnp
from jax import lax
from jax.experimental import pallas as pl
from jax.experimental.pallas import tpu as pltpu
from jax.sharding import Mesh, PartitionSpec as P


NAMES = ("x", "zh", "y", "c", "t")
SIZES = {"x": 4, "zh": 2, "y": 4, "c": 2, "t": 8}
BF16 = jnp.bfloat16
F32 = jnp.float32
ROWS = 128
WIDTH = 256
CHUNK = 3 * ROWS
PARAMS = pltpu.CompilerParams(vmem_limit_bytes=16 << 20)
VMEM = pl.BlockSpec(memory_space=pltpu.VMEM)
SMEM = pl.BlockSpec(memory_space=pltpu.SMEM)


def permutation(names, target):
    pairs = []
    for place in itertools.product(*[range(SIZES[n]) for n in names]):
        goal = target(dict(zip(names, place)))
        source, dest = 0, 0
        for name, coordinate in zip(names, place):
            source = source * SIZES[name] + coordinate
            dest = dest * SIZES[name] + goal[name]
        pairs.append((source, dest))
    return pairs


def permute(values, names, target):
    return lax.ppermute(values, names, permutation(names, target))


def exchange(values, names):
    return lax.all_to_all(values, names, split_axis=0, concat_axis=0)


def to_plane(flip):
    def target(d):
        return {"x": d["t"] // 2, "zh": (d["t"] + flip) % 2, "t": 2 * d["x"] + d["zh"]}

    return target


def gram(values):
    return lax.dot_general(values, values, (((1,), (1,)), ((), ())), preferred_element_type=F32)


def center(values):
    floats = values.astype(F32)
    return (floats - jnp.mean(floats, axis=0, keepdims=True)).astype(BF16)


def source_kernel(acts_ref, partner_ref, out_ref):
    out_ref[:ROWS, :] = center(acts_ref[...])
    out_ref[ROWS:, :] = center(partner_ref[...])


def split(values, parts):
    pieces = []
    for _ in range(parts):
        piece = values.astype(BF16)
        values = values - piece.astype(F32)
        pieces.append(piece)
    return pieces


def chunk_kernel(flag_ref, first_ref, second_ref, chunk_ref):
    even = flag_ref[0] == 0
    first, second = first_ref[...], second_ref[...]
    low = jnp.where(even, first, second)
    high = jnp.where(even, second, first)
    chunk_ref[:ROWS, :] = low[:ROWS]
    chunk_ref[ROWS : 2 * ROWS, :] = high[:ROWS]
    gram_y = gram(jnp.concatenate([low[ROWS:], high[ROWS:]], axis=1))
    chunk_ref[2 * ROWS :, :] = jnp.concatenate(split(gram_y, 2), axis=1)


def gram_kernel(plane_ref, x_ref, y_ref, tiles_ref):
    sums = jnp.zeros((3, ROWS), F32)
    for y in range(0, 4, 2):
        rows = [
            jnp.concatenate(
                [plane_ref[t // 2, y + i, pl.ds((t % 2) * ROWS, ROWS), :] for t in range(8)], axis=1
            )
            for i in range(2)
        ]
        pair = gram(jnp.concatenate(rows, axis=0))
        for i in range(2):
            gram_x = pair[i * ROWS : (i + 1) * ROWS, i * ROWS : (i + 1) * ROWS]
            gram_y = jnp.zeros((ROWS, ROWS), F32)
            for x in range(4):
                parts = plane_ref[x, y + i, pl.ds(2 * ROWS, ROWS), :].astype(F32)
                gram_y = gram_y + (parts[:, :ROWS] + parts[:, ROWS:])
            x_ref[y + i] = gram_x
            y_ref[y + i] = gram_y
            products = (gram_x * gram_x, gram_y * gram_y, gram_x * gram_y)
            sums = sums + jnp.concatenate(
                [jnp.sum(v, axis=0, keepdims=True) for v in products], axis=0
            )
    tile = jnp.concatenate([sums, jnp.zeros((5, ROWS), F32)], axis=0)
    tiles_ref[...] = jnp.broadcast_to(tile[None], tiles_ref.shape)


def plane_grams(plane):
    return pl.pallas_call(
        gram_kernel,
        in_specs=[VMEM],
        out_specs=[VMEM] * 3,
        out_shape=[
            jax.ShapeDtypeStruct((4, ROWS, ROWS), F32),
            jax.ShapeDtypeStruct((4, ROWS, ROWS), F32),
            jax.ShapeDtypeStruct((16, 8, ROWS), F32),
        ],
        compiler_params=PARAMS,
        cost_estimate=pl.CostEstimate(
            flops=2 << 30, bytes_accessed=4 << 20, transcendentals=0
        ),
        name="plane_grams",
    )(plane)


def mix_kernel(
    scale, core_ref, own_x_ref, own_y_ref, other_x_ref, other_y_ref, tiles_ref, hidden_ref,
    mixed_ref, product_ref, cka_ref,
):
    sums = jnp.sum(jnp.sum(tiles_ref[...], axis=0), axis=1, keepdims=True)
    sxx, syy, sxy = sums[0:1], sums[1:2], sums[2:3]
    root = jnp.sqrt(sxx * syy)
    ratio = jnp.broadcast_to(sxy / sxx, (1, ROWS))
    coef = jnp.broadcast_to(-2.0 * scale / root, (1, ROWS))
    cka_ref[...] = jnp.broadcast_to(sxy / root, cka_ref.shape)
    core = core_ref[0]
    for b in range(8):
        x_ref, y_ref = (own_x_ref, own_y_ref) if b < 4 else (other_x_ref, other_y_ref)
        mixed = coef * (y_ref[b % 4] - ratio * x_ref[b % 4])
        mixed_ref[b] = mixed
        place = b % 4 * 2 + (core if b < 4 else 1 - core)
        hidden = hidden_ref[:, pl.ds(pl.multiple_of(place * ROWS, ROWS), ROWS)]
        product = jnp.dot(
            jnp.concatenate([hidden, hidden], axis=1),
            jnp.concatenate(split(mixed, 2), axis=0),
            preferred_element_type=F32,
        )
        product_ref[:, b * ROWS : (b + 1) * ROWS] = product.astype(BF16)


def mix(core, own, other, tiles, hidden, scale):
    return pl.pallas_call(
        functools.partial(mix_kernel, scale),
        in_specs=[SMEM] + [VMEM] * 6,
        out_specs=[VMEM] * 3,
        out_shape=[
            jax.ShapeDtypeStruct((8, ROWS, ROWS), F32),
            jax.ShapeDtypeStruct(hidden.shape, BF16),
            jax.ShapeDtypeStruct((8, ROWS), F32),
        ],
        compiler_params=PARAMS,
        name="mix",
    )(core, own[0], own[1], other[0], other[1], tiles, hidden)


def column_block(place, k):
    return lax.bitwise_xor(place, (k % 2) * 4 + (k // 2 % 2) * 2 + k // 4)


def token_rows(ref, t):
    start = pl.multiple_of(lax.rem(t, 2) * ROWS, ROWS)
    return ref[lax.div(t, 2), :, pl.ds(start, ROWS), :].reshape(4 * ROWS, WIDTH)


def weight_kernel(first, place_ref, product_ref, own_ref, other_ref, out_ref):
    half = 4 * ROWS
    for k in range(4):
        t = column_block(place_ref[0], first + k)
        value = jnp.dot(
            product_ref[:, :half], token_rows(own_ref, t), preferred_element_type=F32
        )
        value = value + jnp.dot(
            product_ref[:, half:], token_rows(other_ref, t), preferred_element_type=F32
        )
        out_ref[k] = value.astype(out_ref.dtype)


def weight_parts(place, product, plane, other, first, dtype):
    units = product.shape[0]
    return pl.pallas_call(
        functools.partial(weight_kernel, first),
        in_specs=[SMEM] + [VMEM] * 3,
        out_specs=VMEM,
        out_shape=jax.ShapeDtypeStruct((4, units, WIDTH), dtype),
        compiler_params=PARAMS,
        cost_estimate=pl.CostEstimate(
            flops=2 * units * 8 * ROWS * 4 * WIDTH, bytes_accessed=4 << 20, transcendentals=0
        ),
        name="weight_parts",
    )(place, product, plane, other)


def hidden_kernel(
    place_ref, core_ref, near_ref, far_ref, own_ref, other_ref, mixed_ref, out_ref
):
    for ref, first in ((own_ref, 0), (other_ref, 4)):
        total = None
        for k in range(8):
            product = lax.dot_general(
                near_ref[k] if k < 4 else far_ref[k - 4],
                token_rows(ref, column_block(place_ref[0], k)),
                (((1,), (1,)), ((), ())),
                preferred_element_type=F32,
            )
            total = product if total is None else total + product
        for y in range(4):
            high, low = split(total[:, y * ROWS : (y + 1) * ROWS], 2)
            mixed_high, mixed_low = split(mixed_ref[first + y], 2)
            value = lax.dot_general(
                jnp.concatenate([high, high, low], axis=1),
                jnp.concatenate([mixed_high, mixed_low, mixed_high], axis=1),
                (((1,), (1,)), ((), ())),
                preferred_element_type=F32,
            )
            place = y * 2 + (core_ref[0] if first == 0 else 1 - core_ref[0])
            out_ref[:, pl.ds(pl.multiple_of(place * ROWS, ROWS), ROWS)] = value.astype(BF16)


def hidden_gradient(place, core, near, far, plane, other, mixed):
    units = near.shape[1]
    tokens = 8 * ROWS
    return pl.pallas_call(
        hidden_kernel,
        in_specs=[SMEM] * 2 + [VMEM] * 5,
        out_specs=VMEM,
        out_shape=jax.ShapeDtypeStruct((units, tokens), BF16),
        compiler_params=PARAMS,
        cost_estimate=pl.CostEstimate(
            flops=2 * units * tokens * 8 * WIDTH, bytes_accessed=8 << 20, transcendentals=0
        ),
        name="hidden_gradient",
    )(place, core, near, far, plane, other, mixed)


def flip(bit):
    return lambda d: {"t": d["t"] ^ bit}


def local(acts, partner, hidden, down_weight):
    scale = float(ROWS * 64 * WIDTH * 8)
    shape = jax.ShapeDtypeStruct
    place = lax.axis_index("t").astype(jnp.int32).reshape(1)
    core = lax.axis_index("c").astype(jnp.int32).reshape(1)
    half = lax.axis_index("zh").astype(jnp.int32).reshape(1)
    near = down_weight[None]
    far = permute(near, ("t",), flip(4))
    near = jnp.concatenate([near, far], axis=0)
    far = permute(near, ("t",), flip(2))
    near = jnp.concatenate([near, far], axis=0)
    far = permute(near, ("t",), flip(1))
    piece = pl.pallas_call(
        source_kernel,
        in_specs=[VMEM] * 2,
        out_specs=VMEM,
        out_shape=shape((2 * ROWS, WIDTH), BF16),
        compiler_params=PARAMS,
        name="source",
    )(acts, partner)
    first = permute(piece, ("x", "zh", "t"), to_plane(0))
    second = permute(piece, ("x", "zh", "t"), to_plane(1))
    chunk = pl.pallas_call(
        chunk_kernel,
        in_specs=[SMEM] + [VMEM] * 2,
        out_specs=VMEM,
        out_shape=shape((CHUNK, WIDTH), BF16),
        compiler_params=PARAMS,
        name="chunk",
    )(half, first, second)
    plane = exchange(jnp.broadcast_to(chunk[None], (16,) + chunk.shape), ("x", "y"))
    other = permute(plane, ("c",), lambda d: {"c": 1 - d["c"]})
    plane = plane.reshape(4, 4, CHUNK, WIDTH)
    other = other.reshape(4, 4, CHUNK, WIDTH)
    own_grams = plane_grams(plane)
    tiles = exchange(own_grams[2], ("c", "t"))
    mixed, product, cka = mix(core, own_grams, plane_grams(other), tiles, hidden, scale)
    sent = weight_parts(place, product, plane, other, 4, BF16)
    sent = permute(sent, ("t",), flip(1))
    kept = weight_parts(place, product, plane, other, 0, F32)
    later = permute((kept[2:] + sent[2:].astype(F32)).astype(BF16), ("t",), flip(2))
    kept = kept[:2] + sent[:2].astype(F32)
    last = permute((kept[1] + later[1].astype(F32)).astype(BF16), ("t",), flip(4))
    grad_weight = kept[0] + later[0].astype(F32) + last.astype(F32)
    grad_hidden = hidden_gradient(place, core, near, far, plane, other, mixed)
    return (grad_hidden, grad_weight, cka[0, 0])


def solution(mesh):
    shape = tuple(SIZES[n] for n in NAMES)
    fine = Mesh(mesh.devices.reshape(shape), NAMES)
    spec = P(("x", "zh", "y", "c"), "t")
    return jax.shard_map(
        local, mesh=fine, in_specs=(spec,) * 4, out_specs=(spec, spec, P()), check_vma=False
    )
```

```python
import functools
import itertools

import jax
import jax.numpy as jnp
from jax import lax
from jax.experimental import pallas as pl
from jax.experimental.pallas import tpu as pltpu
from jax.sharding import Mesh, PartitionSpec as P


NAMES = ("x", "zh", "y", "c", "t")
SIZES = {"x": 4, "zh": 2, "y": 4, "c": 2, "t": 8}
BF16 = jnp.bfloat16
F32 = jnp.float32
ROWS = 128
WIDTH = 256
CHUNK = 3 * ROWS
PARAMS = pltpu.CompilerParams(vmem_limit_bytes=16 << 20)
VMEM = pl.BlockSpec(memory_space=pltpu.VMEM)
SMEM = pl.BlockSpec(memory_space=pltpu.SMEM)


def whole(*shape):
    return pl.BlockSpec(shape, lambda i: (0,) * len(shape))


def permutation(names, target):
    pairs = []
    for place in itertools.product(*[range(SIZES[n]) for n in names]):
        goal = target(dict(zip(names, place)))
        source, dest = 0, 0
        for name, coordinate in zip(names, place):
            source = source * SIZES[name] + coordinate
            dest = dest * SIZES[name] + goal[name]
        pairs.append((source, dest))
    return pairs


def permute(values, names, target):
    return lax.ppermute(values, names, permutation(names, target))


def exchange(values, names):
    return lax.all_to_all(values, names, split_axis=0, concat_axis=0)


def to_plane(flip):
    def target(d):
        return {"x": d["t"] // 2, "zh": (d["t"] + flip) % 2, "t": 2 * d["x"] + d["zh"]}

    return target


def gram(values):
    return lax.dot_general(values, values, (((1,), (1,)), ((), ())), preferred_element_type=F32)


def center(values):
    floats = values.astype(F32)
    return (floats - jnp.mean(floats, axis=0, keepdims=True)).astype(BF16)


def source_kernel(acts_ref, partner_ref, out_ref):
    out_ref[:ROWS, :] = center(acts_ref[...])
    out_ref[ROWS:, :] = center(partner_ref[...])


def split(values, parts):
    pieces = []
    for _ in range(parts):
        piece = values.astype(BF16)
        values = values - piece.astype(F32)
        pieces.append(piece)
    return pieces


def chunk_kernel(flag_ref, first_ref, second_ref, chunk_ref):
    even = flag_ref[0] == 0
    first, second = first_ref[...], second_ref[...]
    low = jnp.where(even, first, second)
    high = jnp.where(even, second, first)
    chunk_ref[:ROWS, :] = low[:ROWS]
    chunk_ref[ROWS : 2 * ROWS, :] = high[:ROWS]
    gram_y = gram(jnp.concatenate([low[ROWS:], high[ROWS:]], axis=1))
    chunk_ref[2 * ROWS :, :] = jnp.concatenate(split(gram_y, 2), axis=1)


def minibatch_grams(plane_ref, first):
    rows = [
        jnp.concatenate(
            [plane_ref[t // 2, first + i, pl.ds((t % 2) * ROWS, ROWS), :] for t in range(8)], axis=1
        )
        for i in range(2)
    ]
    pair = gram(jnp.concatenate(rows, axis=0))
    grams = []
    for i in range(2):
        gram_y = jnp.zeros((ROWS, ROWS), F32)
        for x in range(4):
            parts = plane_ref[x, first + i, pl.ds(2 * ROWS, ROWS), :].astype(F32)
            gram_y = gram_y + (parts[:, :ROWS] + parts[:, ROWS:])
        block = slice(i * ROWS, (i + 1) * ROWS)
        grams.append((pair[block, block], gram_y))
    return grams


def sums_kernel(plane_ref, tiles_ref):
    sums = jnp.zeros((3, ROWS), F32)
    for gram_x, gram_y in minibatch_grams(plane_ref, 0) + minibatch_grams(plane_ref, 2):
        products = (gram_x * gram_x, gram_y * gram_y, gram_x * gram_y)
        sums = sums + jnp.concatenate([jnp.sum(v, axis=0, keepdims=True) for v in products], axis=0)
    tile = jnp.concatenate([sums, jnp.zeros((5, ROWS), F32)], axis=0)
    tiles_ref[...] = jnp.broadcast_to(tile[None], tiles_ref.shape)


def plane_sums(plane):
    return pl.pallas_call(
        sums_kernel,
        in_specs=[VMEM],
        out_specs=VMEM,
        out_shape=jax.ShapeDtypeStruct((16, 8, ROWS), F32),
        compiler_params=PARAMS,
        name="plane_sums",
    )(plane)


def grams_kernel(own_ref, other_ref, grams_ref):
    for base, ref in ((0, own_ref), (4, other_ref)):
        for y in (0, 2):
            for i, (gram_x, gram_y) in enumerate(minibatch_grams(ref, y)):
                grams_ref[0, base + y + i] = gram_x
                grams_ref[1, base + y + i] = gram_y


def plane_grams(plane, other):
    return pl.pallas_call(
        grams_kernel,
        in_specs=[VMEM] * 2,
        out_specs=VMEM,
        out_shape=jax.ShapeDtypeStruct((2, 8, ROWS, ROWS), F32),
        compiler_params=PARAMS,
        cost_estimate=pl.CostEstimate(
            flops=4 << 30, bytes_accessed=8 << 20, transcendentals=0
        ),
        name="plane_grams",
    )(plane, other)


def mix_kernel(
    scale, core_ref, place_ref, grams_ref, tiles_ref, hidden_ref, own_ref, other_ref,
    mixed_ref, product_ref, cka_ref, upper_ref, lower_ref,
):
    sums = jnp.sum(jnp.sum(tiles_ref[...], axis=0), axis=1, keepdims=True)
    sxx, syy, sxy = sums[0:1], sums[1:2], sums[2:3]
    root = jnp.sqrt(sxx * syy)
    ratio = jnp.broadcast_to(sxy / sxx, (1, ROWS))
    coef = jnp.broadcast_to(-2.0 * scale / root, (1, ROWS))
    cka_ref[...] = jnp.broadcast_to(sxy / root, cka_ref.shape)
    core = core_ref[0]
    for b in range(8):
        mixed = coef * (grams_ref[1, b] - ratio * grams_ref[0, b])
        mixed_ref[b] = mixed
        place = b % 4 * 2 + (core if b < 4 else 1 - core)
        hidden = hidden_ref[:, pl.ds(pl.multiple_of(place * ROWS, ROWS), ROWS)]
        product = jnp.dot(
            jnp.concatenate([hidden, hidden], axis=1),
            jnp.concatenate(split(mixed, 2), axis=0),
            preferred_element_type=F32,
        )
        product_ref[:, b * ROWS : (b + 1) * ROWS] = product.astype(BF16)
    middle = upper_ref.shape[1]
    for k in range(4):
        value = weight_block(place_ref, product_ref, own_ref, other_ref, 4 + k).astype(BF16)
        upper_ref[k] = value[:middle]
        lower_ref[k] = value[middle:]


def mix(core, place, grams, tiles, hidden, plane, other, scale):
    units = hidden.shape[0]
    half = jax.ShapeDtypeStruct((4, units // 2, WIDTH), BF16)
    return pl.pallas_call(
        functools.partial(mix_kernel, scale),
        grid=(1,),
        in_specs=[SMEM] * 2
        + [whole(2, 8, ROWS, ROWS), VMEM, whole(*hidden.shape), VMEM, VMEM],
        out_specs=[VMEM] * 5,
        out_shape=[
            jax.ShapeDtypeStruct((8, ROWS, ROWS), F32),
            jax.ShapeDtypeStruct(hidden.shape, BF16),
            jax.ShapeDtypeStruct((8, ROWS), F32),
            half,
            half,
        ],
        compiler_params=PARAMS,
        name="mix",
    )(core, place, grams, tiles, hidden, plane, other)


def column_block(place, k):
    return lax.bitwise_xor(place, (k % 2) * 4 + (k // 2 % 2) * 2 + k // 4)


def token_rows(ref, t):
    start = pl.multiple_of(lax.rem(t, 2) * ROWS, ROWS)
    return ref[lax.div(t, 2), :, pl.ds(start, ROWS), :].reshape(4 * ROWS, WIDTH)


def weight_block(place_ref, product_ref, own_ref, other_ref, k):
    half = 4 * ROWS
    t = column_block(place_ref[0], k)
    value = jnp.dot(product_ref[:, :half], token_rows(own_ref, t), preferred_element_type=F32)
    return value + jnp.dot(
        product_ref[:, half:], token_rows(other_ref, t), preferred_element_type=F32
    )


def weight_kernel(place_ref, product_ref, own_ref, other_ref, out_ref):
    for k in range(4):
        out_ref[k] = weight_block(place_ref, product_ref, own_ref, other_ref, k)


def weight_parts(place, product, plane, other):
    units = product.shape[0]
    return pl.pallas_call(
        weight_kernel,
        in_specs=[SMEM] + [VMEM] * 3,
        out_specs=VMEM,
        out_shape=jax.ShapeDtypeStruct((4, units, WIDTH), F32),
        compiler_params=PARAMS,
        cost_estimate=pl.CostEstimate(
            flops=2 * units * 8 * ROWS * 4 * WIDTH, bytes_accessed=4 << 20, transcendentals=0
        ),
        name="weight_parts",
    )(place, product, plane, other)


def hidden_kernel(
    place_ref, core_ref, near_ref, far_ref, own_ref, other_ref, mixed_ref, out_ref
):
    for ref, first in ((own_ref, 0), (other_ref, 4)):
        total = None
        for k in range(8):
            product = lax.dot_general(
                near_ref[k] if k < 4 else far_ref[k - 4],
                token_rows(ref, column_block(place_ref[0], k)),
                (((1,), (1,)), ((), ())),
                preferred_element_type=F32,
            )
            total = product if total is None else total + product
        for y in range(4):
            high, low = split(total[:, y * ROWS : (y + 1) * ROWS], 2)
            mixed_high, mixed_low = split(mixed_ref[first + y], 2)
            value = lax.dot_general(
                jnp.concatenate([high, high, low], axis=1),
                jnp.concatenate([mixed_high, mixed_low, mixed_high], axis=1),
                (((1,), (1,)), ((), ())),
                preferred_element_type=F32,
            )
            place = y * 2 + (core_ref[0] if first == 0 else 1 - core_ref[0])
            out_ref[:, pl.ds(pl.multiple_of(place * ROWS, ROWS), ROWS)] = value.astype(BF16)


def hidden_gradient(place, core, near, far, plane, other, mixed):
    units = near.shape[1]
    tokens = 8 * ROWS
    return pl.pallas_call(
        hidden_kernel,
        in_specs=[SMEM] * 2 + [VMEM] * 5,
        out_specs=VMEM,
        out_shape=jax.ShapeDtypeStruct((units, tokens), BF16),
        compiler_params=PARAMS,
        cost_estimate=pl.CostEstimate(
            flops=2 * units * tokens * 8 * WIDTH, bytes_accessed=8 << 20, transcendentals=0
        ),
        name="hidden_gradient",
    )(place, core, near, far, plane, other, mixed)


def add_one_kernel(row, kept_ref, arrived_ref, out_ref, moved_ref):
    value = kept_ref[:, row : row + arrived_ref.shape[1]] + arrived_ref[...].astype(F32)
    out_ref[...] = value[:2]
    moved_ref[...] = value[2:].astype(BF16)


def add_one(kept, arrived, half):
    rows = arrived.shape[1]
    return pl.pallas_call(
        functools.partial(add_one_kernel, half * rows),
        in_specs=[VMEM] * 2,
        out_specs=[VMEM] * 2,
        out_shape=[
            jax.ShapeDtypeStruct((2, rows, WIDTH), F32),
            jax.ShapeDtypeStruct((2, rows, WIDTH), BF16),
        ],
        compiler_params=PARAMS,
    )(kept, arrived)


def add_two_kernel(kept_ref, arrived_ref, out_ref, moved_ref):
    value = kept_ref[...] + arrived_ref[...].astype(F32)
    out_ref[...] = value[0]
    moved_ref[...] = value[1].astype(BF16)


def add_two(kept, arrived):
    rows = arrived.shape[1]
    return pl.pallas_call(
        add_two_kernel,
        in_specs=[VMEM] * 2,
        out_specs=[VMEM] * 2,
        out_shape=[
            jax.ShapeDtypeStruct((rows, WIDTH), F32),
            jax.ShapeDtypeStruct((rows, WIDTH), BF16),
        ],
        compiler_params=PARAMS,
    )(kept, arrived)


def add_last_kernel(first_ref, one_ref, second_ref, two_ref, out_ref):
    rows = first_ref.shape[0]
    out_ref[:rows] = first_ref[...] + one_ref[...].astype(F32)
    out_ref[rows:] = second_ref[...] + two_ref[...].astype(F32)


def add_last(*values):
    return pl.pallas_call(
        add_last_kernel,
        in_specs=[VMEM] * 4,
        out_specs=VMEM,
        out_shape=jax.ShapeDtypeStruct((2 * values[0].shape[0], WIDTH), F32),
        compiler_params=PARAMS,
        name="add_last",
    )(*values)


def flip(bit):
    return lambda d: {"t": d["t"] ^ bit}


def local(acts, partner, hidden, down_weight):
    scale = float(ROWS * 64 * WIDTH * 8)
    shape = jax.ShapeDtypeStruct
    place = lax.axis_index("t").astype(jnp.int32).reshape(1)
    core = lax.axis_index("c").astype(jnp.int32).reshape(1)
    half = lax.axis_index("zh").astype(jnp.int32).reshape(1)
    near = down_weight[None]
    far = permute(near, ("t",), flip(4))
    near = jnp.concatenate([near, far], axis=0)
    far = permute(near, ("t",), flip(2))
    near = jnp.concatenate([near, far], axis=0)
    far = permute(near, ("t",), flip(1))
    piece = pl.pallas_call(
        source_kernel,
        grid=(1,),
        in_specs=[whole(ROWS, WIDTH)] * 2,
        out_specs=VMEM,
        out_shape=shape((2 * ROWS, WIDTH), BF16),
        compiler_params=PARAMS,
        name="source",
    )(acts, partner)
    first = permute(piece, ("x", "zh", "t"), to_plane(0))
    second = permute(piece, ("x", "zh", "t"), to_plane(1))
    chunk = pl.pallas_call(
        chunk_kernel,
        in_specs=[SMEM] + [VMEM] * 2,
        out_specs=VMEM,
        out_shape=shape((CHUNK, WIDTH), BF16),
        compiler_params=PARAMS,
        name="chunk",
    )(half, first, second)
    plane = exchange(jnp.broadcast_to(chunk[None], (16,) + chunk.shape), ("x", "y"))
    other = permute(plane, ("c",), lambda d: {"c": 1 - d["c"]})
    plane = plane.reshape(4, 4, CHUNK, WIDTH)
    other = other.reshape(4, 4, CHUNK, WIDTH)
    tiles = exchange(plane_sums(plane), ("c", "t"))
    grams = plane_grams(plane, other)
    mixed, product, cka, *sent = mix(core, place, grams, tiles, hidden, plane, other, scale)
    arrived, later, last = {}, {}, {}
    for name, values in zip("ab", sent):
        arrived[name] = permute(values, ("t",), flip(1))
    kept = weight_parts(place, product, plane, other)
    halves = {}
    for i, name in enumerate("ab"):
        halves[name], moved = add_one(kept, arrived[name], i)
        later[name] = permute(moved, ("t",), flip(2))
    for name in "ab":
        halves[name], moved = add_two(halves[name], later[name])
        last[name] = permute(moved, ("t",), flip(4))
    grad_weight = add_last(halves["a"], last["a"], halves["b"], last["b"])
    grad_hidden = hidden_gradient(place, core, near, far, plane, other, mixed)
    return (grad_hidden, grad_weight, cka[0, 0])


def solution(mesh):
    shape = tuple(SIZES[n] for n in NAMES)
    fine = Mesh(mesh.devices.reshape(shape), NAMES)
    spec = P(("x", "zh", "y", "c"), "t")
    return jax.shard_map(
        local, mesh=fine, in_specs=(spec,) * 4, out_specs=(spec, spec, P()), check_vma=False
    )
```

```python
import functools
import itertools

import jax
import jax.numpy as jnp
from jax import lax
from jax.experimental import pallas as pl
from jax.experimental.pallas import tpu as pltpu
from jax.sharding import Mesh, PartitionSpec as P


NAMES = ("x", "zh", "y", "c", "t")
SIZES = {"x": 4, "zh": 2, "y": 4, "c": 2, "t": 8}
BF16 = jnp.bfloat16
F32 = jnp.float32
ROWS = 128
WIDTH = 256
HALF = ROWS // 2
PACKED = HALF + HALF // 2
PIECE = ROWS + PACKED
CHUNK = 2 * ROWS + PACKED
PARAMS = pltpu.CompilerParams(vmem_limit_bytes=16 << 20)
VMEM = pl.BlockSpec(memory_space=pltpu.VMEM)
SMEM = pl.BlockSpec(memory_space=pltpu.SMEM)


def whole(*shape):
    return pl.BlockSpec(shape, lambda i: (0,) * len(shape))


def permutation(names, target):
    pairs = []
    for place in itertools.product(*[range(SIZES[n]) for n in names]):
        goal = target(dict(zip(names, place)))
        source, dest = 0, 0
        for name, coordinate in zip(names, place):
            source = source * SIZES[name] + coordinate
            dest = dest * SIZES[name] + goal[name]
        pairs.append((source, dest))
    return pairs


def permute(values, names, target):
    return lax.ppermute(values, names, permutation(names, target))


def exchange(values, names):
    return lax.all_to_all(values, names, split_axis=0, concat_axis=0)


def to_plane(flip):
    def target(d):
        return {"x": d["t"] // 2, "zh": (d["t"] + flip) % 2, "t": 2 * d["x"] + d["zh"]}

    return target


def gram(values):
    return lax.dot_general(values, values, (((1,), (1,)), ((), ())), preferred_element_type=F32)


def center(values):
    floats = values.astype(F32)
    return (floats - jnp.mean(floats, axis=0, keepdims=True)).astype(BF16)


def split(values, parts):
    pieces = []
    for _ in range(parts):
        piece = values.astype(BF16)
        values = values - piece.astype(F32)
        pieces.append(piece)
    return pieces


def left(rows):
    return lax.broadcasted_iota(jnp.int32, (rows, ROWS), 1) < HALF


def pack(values):
    top, bottom = values[:HALF], values[HALF:]
    corner = jnp.where(
        left(HALF // 2), pltpu.roll(top[: HALF // 2], HALF, 1), top[HALF // 2 :]
    )
    return jnp.concatenate([jnp.where(left(HALF), top, bottom), corner], axis=0)


def unpack(packed):
    blocks, corner = packed[:HALF], packed[HALF:]
    right = jnp.concatenate([pltpu.roll(corner, HALF, 1), corner], axis=0)
    upper = jnp.concatenate([jnp.where(left(HALF), blocks, right), blocks], axis=0)
    below = lax.broadcasted_iota(jnp.int32, (ROWS, ROWS), 0) >= HALF
    return jnp.where(jnp.logical_and(below, left(ROWS)), upper.T, upper)


def two_parts(values):
    return jnp.concatenate(split(values, 2), axis=1)


def joined(parts):
    parts = parts.astype(F32)
    return parts[:, :ROWS] + parts[:, ROWS:]


def source_kernel(acts_ref, partner_ref, out_ref):
    out_ref[:ROWS, :] = center(acts_ref[...])
    out_ref[ROWS:, :] = two_parts(pack(gram(center(partner_ref[...]))))


def chunk_kernel(flag_ref, first_ref, second_ref, chunk_ref):
    even = flag_ref[0] == 0
    first, second = first_ref[:ROWS, :], second_ref[:ROWS, :]
    chunk_ref[:ROWS, :] = jnp.where(even, first, second)
    chunk_ref[ROWS : 2 * ROWS, :] = jnp.where(even, second, first)
    chunk_ref[2 * ROWS :, :] = two_parts(joined(first_ref[ROWS:, :]) + joined(second_ref[ROWS:, :]))


def minibatch_grams(plane_ref, first):
    rows = [
        jnp.concatenate(
            [plane_ref[t // 2, first + i, pl.ds((t % 2) * ROWS, ROWS), :] for t in range(8)], axis=1
        )
        for i in range(2)
    ]
    pair = gram(jnp.concatenate(rows, axis=0))
    grams = []
    for i in range(2):
        packed = jnp.zeros((PACKED, ROWS), F32)
        for x in range(4):
            packed = packed + joined(plane_ref[x, first + i, pl.ds(2 * ROWS, PACKED), :])
        block = slice(i * ROWS, (i + 1) * ROWS)
        grams.append((pair[block, block], unpack(packed)))
    return grams


def sums_kernel(plane_ref, tiles_ref):
    sums = jnp.zeros((3, ROWS), F32)
    for gram_x, gram_y in minibatch_grams(plane_ref, 0) + minibatch_grams(plane_ref, 2):
        products = (gram_x * gram_x, gram_y * gram_y, gram_x * gram_y)
        sums = sums + jnp.concatenate([jnp.sum(v, axis=0, keepdims=True) for v in products], axis=0)
    tile = jnp.concatenate([sums, jnp.zeros((5, ROWS), F32)], axis=0)
    tiles_ref[...] = jnp.broadcast_to(tile[None], tiles_ref.shape)


def plane_sums(plane):
    return pl.pallas_call(
        sums_kernel,
        in_specs=[VMEM],
        out_specs=VMEM,
        out_shape=jax.ShapeDtypeStruct((16, 8, ROWS), F32),
        compiler_params=PARAMS,
        name="plane_sums",
    )(plane)


def grams_kernel(own_ref, other_ref, grams_ref):
    for base, ref in ((0, own_ref), (4, other_ref)):
        for y in (0, 2):
            for i, (gram_x, gram_y) in enumerate(minibatch_grams(ref, y)):
                grams_ref[0, base + y + i] = gram_x
                grams_ref[1, base + y + i] = gram_y


def plane_grams(plane, other):
    return pl.pallas_call(
        grams_kernel,
        in_specs=[VMEM] * 2,
        out_specs=VMEM,
        out_shape=jax.ShapeDtypeStruct((2, 8, ROWS, ROWS), F32),
        compiler_params=PARAMS,
        cost_estimate=pl.CostEstimate(
            flops=4 << 30, bytes_accessed=8 << 20, transcendentals=0
        ),
        name="plane_grams",
    )(plane, other)


def mix_kernel(
    scale, core_ref, place_ref, grams_ref, tiles_ref, hidden_ref, own_ref, other_ref,
    mixed_ref, product_ref, cka_ref, upper_ref, lower_ref,
):
    sums = jnp.sum(jnp.sum(tiles_ref[...], axis=0), axis=1, keepdims=True)
    sxx, syy, sxy = sums[0:1], sums[1:2], sums[2:3]
    root = jnp.sqrt(sxx * syy)
    ratio = jnp.broadcast_to(sxy / sxx, (1, ROWS))
    coef = jnp.broadcast_to(-2.0 * scale / root, (1, ROWS))
    cka_ref[...] = jnp.broadcast_to(sxy / root, cka_ref.shape)
    core = core_ref[0]
    for b in range(8):
        mixed = coef * (grams_ref[1, b] - ratio * grams_ref[0, b])
        mixed_ref[b] = mixed
        place = b % 4 * 2 + (core if b < 4 else 1 - core)
        hidden = hidden_ref[:, pl.ds(pl.multiple_of(place * ROWS, ROWS), ROWS)]
        product = jnp.dot(
            jnp.concatenate([hidden, hidden], axis=1),
            jnp.concatenate(split(mixed, 2), axis=0),
            preferred_element_type=F32,
        )
        product_ref[:, b * ROWS : (b + 1) * ROWS] = product.astype(BF16)
    middle = upper_ref.shape[1]
    for k in range(4):
        value = weight_block(place_ref, product_ref, own_ref, other_ref, 4 + k).astype(BF16)
        upper_ref[k] = value[:middle]
        lower_ref[k] = value[middle:]


def mix(core, place, grams, tiles, hidden, plane, other, scale):
    units = hidden.shape[0]
    half = jax.ShapeDtypeStruct((4, units // 2, WIDTH), BF16)
    return pl.pallas_call(
        functools.partial(mix_kernel, scale),
        grid=(1,),
        in_specs=[SMEM] * 2
        + [whole(2, 8, ROWS, ROWS), VMEM, whole(*hidden.shape), VMEM, VMEM],
        out_specs=[VMEM] * 5,
        out_shape=[
            jax.ShapeDtypeStruct((8, ROWS, ROWS), F32),
            jax.ShapeDtypeStruct(hidden.shape, BF16),
            jax.ShapeDtypeStruct((8, ROWS), F32),
            half,
            half,
        ],
        compiler_params=PARAMS,
        name="mix",
    )(core, place, grams, tiles, hidden, plane, other)


def column_block(place, k):
    return lax.bitwise_xor(place, (k % 2) * 4 + (k // 2 % 2) * 2 + k // 4)


def token_rows(ref, t):
    start = pl.multiple_of(lax.rem(t, 2) * ROWS, ROWS)
    return ref[lax.div(t, 2), :, pl.ds(start, ROWS), :].reshape(4 * ROWS, WIDTH)


def weight_block(place_ref, product_ref, own_ref, other_ref, k):
    half = 4 * ROWS
    t = column_block(place_ref[0], k)
    value = jnp.dot(product_ref[:, :half], token_rows(own_ref, t), preferred_element_type=F32)
    return value + jnp.dot(
        product_ref[:, half:], token_rows(other_ref, t), preferred_element_type=F32
    )


def weight_kernel(place_ref, product_ref, own_ref, other_ref, out_ref):
    for k in range(4):
        out_ref[k] = weight_block(place_ref, product_ref, own_ref, other_ref, k)


def weight_parts(place, product, plane, other):
    units = product.shape[0]
    return pl.pallas_call(
        weight_kernel,
        in_specs=[SMEM] + [VMEM] * 3,
        out_specs=VMEM,
        out_shape=jax.ShapeDtypeStruct((4, units, WIDTH), F32),
        compiler_params=PARAMS,
        cost_estimate=pl.CostEstimate(
            flops=2 * units * 8 * ROWS * 4 * WIDTH, bytes_accessed=4 << 20, transcendentals=0
        ),
        name="weight_parts",
    )(place, product, plane, other)


def hidden_kernel(
    place_ref, core_ref, near_ref, far_ref, own_ref, other_ref, mixed_ref, out_ref
):
    for ref, first in ((own_ref, 0), (other_ref, 4)):
        total = None
        for k in range(8):
            product = lax.dot_general(
                near_ref[k] if k < 4 else far_ref[k - 4],
                token_rows(ref, column_block(place_ref[0], k)),
                (((1,), (1,)), ((), ())),
                preferred_element_type=F32,
            )
            total = product if total is None else total + product
        for y in range(4):
            high, low = split(total[:, y * ROWS : (y + 1) * ROWS], 2)
            mixed_high, mixed_low = split(mixed_ref[first + y], 2)
            value = lax.dot_general(
                jnp.concatenate([high, high, low], axis=1),
                jnp.concatenate([mixed_high, mixed_low, mixed_high], axis=1),
                (((1,), (1,)), ((), ())),
                preferred_element_type=F32,
            )
            place = y * 2 + (core_ref[0] if first == 0 else 1 - core_ref[0])
            out_ref[:, pl.ds(pl.multiple_of(place * ROWS, ROWS), ROWS)] = value.astype(BF16)


def hidden_gradient(place, core, near, far, plane, other, mixed):
    units = near.shape[1]
    tokens = 8 * ROWS
    return pl.pallas_call(
        hidden_kernel,
        in_specs=[SMEM] * 2 + [VMEM] * 5,
        out_specs=VMEM,
        out_shape=jax.ShapeDtypeStruct((units, tokens), BF16),
        compiler_params=PARAMS,
        cost_estimate=pl.CostEstimate(
            flops=2 * units * tokens * 8 * WIDTH, bytes_accessed=8 << 20, transcendentals=0
        ),
        name="hidden_gradient",
    )(place, core, near, far, plane, other, mixed)


def add_one_kernel(row, kept_ref, arrived_ref, out_ref, moved_ref):
    value = kept_ref[:, row : row + arrived_ref.shape[1]] + arrived_ref[...].astype(F32)
    out_ref[...] = value[:2]
    moved_ref[...] = value[2:].astype(BF16)


def add_one(kept, arrived, half):
    rows = arrived.shape[1]
    return pl.pallas_call(
        functools.partial(add_one_kernel, half * rows),
        in_specs=[VMEM] * 2,
        out_specs=[VMEM] * 2,
        out_shape=[
            jax.ShapeDtypeStruct((2, rows, WIDTH), F32),
            jax.ShapeDtypeStruct((2, rows, WIDTH), BF16),
        ],
        compiler_params=PARAMS,
    )(kept, arrived)


def add_two_kernel(kept_ref, arrived_ref, out_ref, moved_ref):
    value = kept_ref[...] + arrived_ref[...].astype(F32)
    out_ref[...] = value[0]
    moved_ref[...] = value[1].astype(BF16)


def add_two(kept, arrived):
    rows = arrived.shape[1]
    return pl.pallas_call(
        add_two_kernel,
        in_specs=[VMEM] * 2,
        out_specs=[VMEM] * 2,
        out_shape=[
            jax.ShapeDtypeStruct((rows, WIDTH), F32),
            jax.ShapeDtypeStruct((rows, WIDTH), BF16),
        ],
        compiler_params=PARAMS,
    )(kept, arrived)


def add_last_kernel(first_ref, one_ref, second_ref, two_ref, out_ref):
    rows = first_ref.shape[0]
    out_ref[:rows] = first_ref[...] + one_ref[...].astype(F32)
    out_ref[rows:] = second_ref[...] + two_ref[...].astype(F32)


def add_last(*values):
    return pl.pallas_call(
        add_last_kernel,
        in_specs=[VMEM] * 4,
        out_specs=VMEM,
        out_shape=jax.ShapeDtypeStruct((2 * values[0].shape[0], WIDTH), F32),
        compiler_params=PARAMS,
        name="add_last",
    )(*values)


def flip(bit):
    return lambda d: {"t": d["t"] ^ bit}


def local(acts, partner, hidden, down_weight):
    scale = float(ROWS * 64 * WIDTH * 8)
    shape = jax.ShapeDtypeStruct
    place = lax.axis_index("t").astype(jnp.int32).reshape(1)
    core = lax.axis_index("c").astype(jnp.int32).reshape(1)
    half = lax.axis_index("zh").astype(jnp.int32).reshape(1)
    near = down_weight[None]
    far = permute(near, ("t",), flip(4))
    near = jnp.concatenate([near, far], axis=0)
    far = permute(near, ("t",), flip(2))
    near = jnp.concatenate([near, far], axis=0)
    far = permute(near, ("t",), flip(1))
    piece = pl.pallas_call(
        source_kernel,
        grid=(1,),
        in_specs=[whole(ROWS, WIDTH)] * 2,
        out_specs=VMEM,
        out_shape=shape((PIECE, WIDTH), BF16),
        compiler_params=PARAMS,
        name="source",
    )(acts, partner)
    first = permute(piece, ("x", "zh", "t"), to_plane(0))
    second = permute(piece, ("x", "zh", "t"), to_plane(1))
    chunk = pl.pallas_call(
        chunk_kernel,
        in_specs=[SMEM] + [VMEM] * 2,
        out_specs=VMEM,
        out_shape=shape((CHUNK, WIDTH), BF16),
        compiler_params=PARAMS,
        name="chunk",
    )(half, first, second)
    plane = exchange(jnp.broadcast_to(chunk[None], (16,) + chunk.shape), ("x", "y"))
    other = permute(plane, ("c",), lambda d: {"c": 1 - d["c"]})
    plane = plane.reshape(4, 4, CHUNK, WIDTH)
    other = other.reshape(4, 4, CHUNK, WIDTH)
    tiles = exchange(plane_sums(plane), ("c", "t"))
    grams = plane_grams(plane, other)
    mixed, product, cka, *sent = mix(core, place, grams, tiles, hidden, plane, other, scale)
    arrived, later, last = {}, {}, {}
    for name, values in zip("ab", sent):
        arrived[name] = permute(values, ("t",), flip(1))
    kept = weight_parts(place, product, plane, other)
    halves = {}
    for i, name in enumerate("ab"):
        halves[name], moved = add_one(kept, arrived[name], i)
        later[name] = permute(moved, ("t",), flip(2))
    for name in "ab":
        halves[name], moved = add_two(halves[name], later[name])
        last[name] = permute(moved, ("t",), flip(4))
    grad_weight = add_last(halves["a"], last["a"], halves["b"], last["b"])
    grad_hidden = hidden_gradient(place, core, near, far, plane, other, mixed)
    return (grad_hidden, grad_weight, cka[0, 0])


def solution(mesh):
    shape = tuple(SIZES[n] for n in NAMES)
    fine = Mesh(mesh.devices.reshape(shape), NAMES)
    spec = P(("x", "zh", "y", "c"), "t")
    return jax.shard_map(
        local, mesh=fine, in_specs=(spec,) * 4, out_specs=(spec, spec, P()), check_vma=False
    )
```

```python
import functools
import itertools

import jax
import jax.numpy as jnp
from jax import lax
from jax.experimental import pallas as pl
from jax.experimental.pallas import tpu as pltpu
from jax.sharding import Mesh, PartitionSpec as P


NAMES = ("x", "zh", "y", "c", "t")
SIZES = {"x": 4, "zh": 2, "y": 4, "c": 2, "t": 8}
BF16 = jnp.bfloat16
F32 = jnp.float32
ROWS = 128
WIDTH = 256
HALF = ROWS // 2
PACKED = HALF + HALF // 2
PIECE = ROWS + PACKED
CHUNK = 2 * ROWS + PACKED
PARAMS = pltpu.CompilerParams(vmem_limit_bytes=16 << 20)
VMEM = pl.BlockSpec(memory_space=pltpu.VMEM)
SMEM = pl.BlockSpec(memory_space=pltpu.SMEM)
HBM = pl.BlockSpec(memory_space=pltpu.HBM)


def permutation(names, target):
    pairs = []
    for place in itertools.product(*[range(SIZES[n]) for n in names]):
        goal = target(dict(zip(names, place)))
        source, dest = 0, 0
        for name, coordinate in zip(names, place):
            source = source * SIZES[name] + coordinate
            dest = dest * SIZES[name] + goal[name]
        pairs.append((source, dest))
    return pairs


def permute(values, names, target):
    return lax.ppermute(values, names, permutation(names, target))


def exchange(values, names):
    return lax.all_to_all(values, names, split_axis=0, concat_axis=0)


def to_plane(flip):
    def target(d):
        return {"x": d["t"] // 2, "zh": (d["t"] + flip) % 2, "t": 2 * d["x"] + d["zh"]}

    return target


def gram(values):
    return lax.dot_general(values, values, (((1,), (1,)), ((), ())), preferred_element_type=F32)


def center(values):
    floats = values.astype(F32)
    return (floats - jnp.mean(floats, axis=0, keepdims=True)).astype(BF16)


def split(values, parts):
    pieces = []
    for _ in range(parts):
        piece = values.astype(BF16)
        values = values - piece.astype(F32)
        pieces.append(piece)
    return pieces


def left(rows):
    return lax.broadcasted_iota(jnp.int32, (rows, ROWS), 1) < HALF


def pack(values):
    top, bottom = values[:HALF], values[HALF:]
    corner = jnp.where(
        left(HALF // 2), pltpu.roll(top[: HALF // 2], HALF, 1), top[HALF // 2 :]
    )
    return jnp.concatenate([jnp.where(left(HALF), top, bottom), corner], axis=0)


def unpack(packed):
    blocks, corner = packed[:HALF], packed[HALF:]
    right = jnp.concatenate([pltpu.roll(corner, HALF, 1), corner], axis=0)
    upper = jnp.concatenate([jnp.where(left(HALF), blocks, right), blocks], axis=0)
    below = lax.broadcasted_iota(jnp.int32, (ROWS, ROWS), 0) >= HALF
    return jnp.where(jnp.logical_and(below, left(ROWS)), upper.T, upper)


def two_parts(values):
    return jnp.concatenate(split(values, 2), axis=1)


def joined(parts):
    parts = parts.astype(F32)
    return parts[:, :ROWS] + parts[:, ROWS:]


def in_hbm(values):
    return pltpu.with_memory_space_constraint(values, pltpu.HBM)


def fetch(source, target, semaphores, i):
    copy = pltpu.make_async_copy(source, target, semaphores.at[i])
    copy.start()
    return copy


def source_kernel(acts_hbm, partner_hbm, out_ref, acts_ref, partner_ref, semaphores):
    partner = fetch(partner_hbm, partner_ref, semaphores, 0)
    acts = fetch(acts_hbm, acts_ref, semaphores, 1)
    partner.wait()
    out_ref[ROWS:, :] = two_parts(pack(gram(center(partner_ref[...]))))
    acts.wait()
    out_ref[:ROWS, :] = center(acts_ref[...])


def chunk_kernel(flag_ref, first_ref, second_ref, chunk_ref):
    even = flag_ref[0] == 0
    first, second = first_ref[:ROWS, :], second_ref[:ROWS, :]
    chunk_ref[:ROWS, :] = jnp.where(even, first, second)
    chunk_ref[ROWS : 2 * ROWS, :] = jnp.where(even, second, first)
    chunk_ref[2 * ROWS :, :] = two_parts(joined(first_ref[ROWS:, :]) + joined(second_ref[ROWS:, :]))


def minibatch_grams(plane_ref, first):
    rows = [
        jnp.concatenate(
            [plane_ref[t // 2, first + i, pl.ds((t % 2) * ROWS, ROWS), :] for t in range(8)], axis=1
        )
        for i in range(2)
    ]
    pair = gram(jnp.concatenate(rows, axis=0))
    grams = []
    for i in range(2):
        packed = jnp.zeros((PACKED, ROWS), F32)
        for x in range(4):
            packed = packed + joined(plane_ref[x, first + i, pl.ds(2 * ROWS, PACKED), :])
        block = slice(i * ROWS, (i + 1) * ROWS)
        grams.append((pair[block, block], unpack(packed)))
    return grams


def sums_kernel(plane_ref, tiles_ref):
    sums = jnp.zeros((3, ROWS), F32)
    for gram_x, gram_y in minibatch_grams(plane_ref, 0) + minibatch_grams(plane_ref, 2):
        products = (gram_x * gram_x, gram_y * gram_y, gram_x * gram_y)
        sums = sums + jnp.concatenate([jnp.sum(v, axis=0, keepdims=True) for v in products], axis=0)
    tile = jnp.concatenate([sums, jnp.zeros((5, ROWS), F32)], axis=0)
    tiles_ref[...] = jnp.broadcast_to(tile[None], tiles_ref.shape)


def plane_sums(plane):
    return pl.pallas_call(
        sums_kernel,
        in_specs=[VMEM],
        out_specs=VMEM,
        out_shape=jax.ShapeDtypeStruct((16, 8, ROWS), F32),
        compiler_params=PARAMS,
        name="plane_sums",
    )(plane)


def mix_kernel(
    scale, core_ref, place_ref, tiles_ref, own_ref, hidden_hbm, other_hbm,
    mixed_ref, product_ref, cka_ref, upper_ref, lower_ref, hidden_ref, other_ref, semaphores,
):
    other_copy = fetch(other_hbm, other_ref, semaphores, 0)
    hidden_copy = fetch(hidden_hbm, hidden_ref, semaphores, 1)
    sums = jnp.sum(jnp.sum(tiles_ref[...], axis=0), axis=1, keepdims=True)
    sxx, syy, sxy = sums[0:1], sums[1:2], sums[2:3]
    root = jnp.sqrt(sxx * syy)
    ratio = jnp.broadcast_to(sxy / sxx, (1, ROWS))
    coef = jnp.broadcast_to(-2.0 * scale / root, (1, ROWS))
    cka_ref[...] = jnp.broadcast_to(sxy / root, cka_ref.shape)
    core = core_ref[0]

    def mix_pair(ref, base, first):
        for i, (gram_x, gram_y) in enumerate(minibatch_grams(ref, first)):
            mixed_ref[base + first + i] = coef * (gram_y - ratio * gram_x)

    mix_pair(own_ref, 0, 0)
    mix_pair(own_ref, 0, 2)
    other_copy.wait()
    mix_pair(other_ref, 4, 0)
    mix_pair(other_ref, 4, 2)
    hidden_copy.wait()
    for b in range(8):
        place = b % 4 * 2 + (core if b < 4 else 1 - core)
        hidden = hidden_ref[:, pl.ds(pl.multiple_of(place * ROWS, ROWS), ROWS)]
        product = jnp.dot(
            jnp.concatenate([hidden, hidden], axis=1),
            jnp.concatenate(split(mixed_ref[b], 2), axis=0),
            preferred_element_type=F32,
        )
        product_ref[:, b * ROWS : (b + 1) * ROWS] = product.astype(BF16)
    middle = upper_ref.shape[1]
    for k in range(4):
        value = weight_block(place_ref, product_ref, own_ref, other_ref, 4 + k).astype(BF16)
        upper_ref[k] = value[:middle]
        lower_ref[k] = value[middle:]


def mix(core, place, tiles, hidden, plane, other, scale):
    units = hidden.shape[0]
    half = jax.ShapeDtypeStruct((4, units // 2, WIDTH), BF16)
    return pl.pallas_call(
        functools.partial(mix_kernel, scale),
        in_specs=[SMEM] * 2 + [VMEM] * 2 + [HBM] * 2,
        out_specs=[VMEM] * 5,
        out_shape=[
            jax.ShapeDtypeStruct((8, ROWS, ROWS), F32),
            jax.ShapeDtypeStruct(hidden.shape, BF16),
            jax.ShapeDtypeStruct((8, ROWS), F32),
            half,
            half,
        ],
        scratch_shapes=[
            pltpu.VMEM(hidden.shape, BF16),
            pltpu.VMEM(other.shape, BF16),
            pltpu.SemaphoreType.DMA((2,)),
        ],
        compiler_params=PARAMS,
        name="mix",
    )(core, place, tiles, plane, in_hbm(hidden), other)


def column_block(place, k):
    return lax.bitwise_xor(place, (k % 2) * 4 + (k // 2 % 2) * 2 + k // 4)


def token_rows(ref, t):
    start = pl.multiple_of(lax.rem(t, 2) * ROWS, ROWS)
    return ref[lax.div(t, 2), :, pl.ds(start, ROWS), :].reshape(4 * ROWS, WIDTH)


def weight_block(place_ref, product_ref, own_ref, other_ref, k):
    half = 4 * ROWS
    t = column_block(place_ref[0], k)
    value = jnp.dot(product_ref[:, :half], token_rows(own_ref, t), preferred_element_type=F32)
    return value + jnp.dot(
        product_ref[:, half:], token_rows(other_ref, t), preferred_element_type=F32
    )


def weight_kernel(place_ref, product_ref, own_ref, other_ref, out_ref):
    for k in range(4):
        out_ref[k] = weight_block(place_ref, product_ref, own_ref, other_ref, k)


def weight_parts(place, product, plane, other):
    units = product.shape[0]
    return pl.pallas_call(
        weight_kernel,
        in_specs=[SMEM] + [VMEM] * 3,
        out_specs=VMEM,
        out_shape=jax.ShapeDtypeStruct((4, units, WIDTH), F32),
        compiler_params=PARAMS,
        cost_estimate=pl.CostEstimate(
            flops=2 * units * 8 * ROWS * 4 * WIDTH, bytes_accessed=4 << 20, transcendentals=0
        ),
        name="weight_parts",
    )(place, product, plane, other)


def hidden_kernel(
    place_ref, core_ref, near_ref, two_ref, one_ref, three_ref, own_ref, mixed_ref, other_hbm,
    out_ref, other_ref, semaphores,
):
    other_copy = fetch(other_hbm, other_ref, semaphores, 0)
    weights = [ref[i] for ref in (near_ref, two_ref, one_ref, three_ref) for i in range(2)]
    for ref, first in ((own_ref, 0), (other_ref, 4)):
        if first == 4:
            other_copy.wait()
        total = None
        for k in range(8):
            product = lax.dot_general(
                weights[k],
                token_rows(ref, column_block(place_ref[0], k)),
                (((1,), (1,)), ((), ())),
                preferred_element_type=F32,
            )
            total = product if total is None else total + product
        for y in range(4):
            high, low = split(total[:, y * ROWS : (y + 1) * ROWS], 2)
            mixed_high, mixed_low = split(mixed_ref[first + y], 2)
            value = lax.dot_general(
                jnp.concatenate([high, high, low], axis=1),
                jnp.concatenate([mixed_high, mixed_low, mixed_high], axis=1),
                (((1,), (1,)), ((), ())),
                preferred_element_type=F32,
            )
            place = y * 2 + (core_ref[0] if first == 0 else 1 - core_ref[0])
            out_ref[:, pl.ds(pl.multiple_of(place * ROWS, ROWS), ROWS)] = value.astype(BF16)


def hidden_gradient(place, core, weights, plane, other, mixed):
    units = weights[0].shape[1]
    tokens = 8 * ROWS
    return pl.pallas_call(
        hidden_kernel,
        in_specs=[SMEM] * 2 + [VMEM] * 6 + [HBM],
        out_specs=VMEM,
        out_shape=jax.ShapeDtypeStruct((units, tokens), BF16),
        scratch_shapes=[pltpu.VMEM(other.shape, BF16), pltpu.SemaphoreType.DMA((1,))],
        compiler_params=PARAMS,
        cost_estimate=pl.CostEstimate(
            flops=2 * units * tokens * 8 * WIDTH, bytes_accessed=8 << 20, transcendentals=0
        ),
        name="hidden_gradient",
    )(place, core, *weights, plane, mixed, other)


def add_one_kernel(row, kept_ref, arrived_ref, out_ref, moved_ref):
    value = kept_ref[:, row : row + arrived_ref.shape[1]] + arrived_ref[...].astype(F32)
    out_ref[...] = value[:2]
    moved_ref[...] = value[2:].astype(BF16)


def add_one(kept, arrived, half):
    rows = arrived.shape[1]
    return pl.pallas_call(
        functools.partial(add_one_kernel, half * rows),
        in_specs=[VMEM] * 2,
        out_specs=[VMEM] * 2,
        out_shape=[
            jax.ShapeDtypeStruct((2, rows, WIDTH), F32),
            jax.ShapeDtypeStruct((2, rows, WIDTH), BF16),
        ],
        compiler_params=PARAMS,
    )(kept, arrived)


def add_two_kernel(kept_ref, arrived_ref, out_ref, moved_ref):
    value = kept_ref[...] + arrived_ref[...].astype(F32)
    out_ref[...] = value[0]
    moved_ref[...] = value[1].astype(BF16)


def add_two(kept, arrived):
    rows = arrived.shape[1]
    return pl.pallas_call(
        add_two_kernel,
        in_specs=[VMEM] * 2,
        out_specs=[VMEM] * 2,
        out_shape=[
            jax.ShapeDtypeStruct((rows, WIDTH), F32),
            jax.ShapeDtypeStruct((rows, WIDTH), BF16),
        ],
        compiler_params=PARAMS,
    )(kept, arrived)


def add_last_kernel(first_ref, one_ref, second_ref, two_ref, out_ref):
    rows = first_ref.shape[0]
    out_ref[:rows] = first_ref[...] + one_ref[...].astype(F32)
    out_ref[rows:] = second_ref[...] + two_ref[...].astype(F32)


def add_last(*values):
    return pl.pallas_call(
        add_last_kernel,
        in_specs=[VMEM] * 4,
        out_specs=VMEM,
        out_shape=jax.ShapeDtypeStruct((2 * values[0].shape[0], WIDTH), F32),
        compiler_params=PARAMS,
        name="add_last",
    )(*values)


def flip(bit):
    return lambda d: {"t": d["t"] ^ bit}


def local(acts, partner, hidden, down_weight):
    scale = float(ROWS * 64 * WIDTH * 8)
    shape = jax.ShapeDtypeStruct
    place = lax.axis_index("t").astype(jnp.int32).reshape(1)
    core = lax.axis_index("c").astype(jnp.int32).reshape(1)
    half = lax.axis_index("zh").astype(jnp.int32).reshape(1)
    near = down_weight[None]
    far = permute(near, ("t",), flip(4))
    near = jnp.concatenate([near, far], axis=0)
    weights = [near]
    for bit in (2, 1, 3):
        weights.append(permute(near, ("t",), flip(bit)))
    piece = pl.pallas_call(
        source_kernel,
        in_specs=[HBM] * 2,
        out_specs=VMEM,
        scratch_shapes=[pltpu.VMEM((ROWS, WIDTH), BF16)] * 2 + [pltpu.SemaphoreType.DMA((2,))],
        out_shape=shape((PIECE, WIDTH), BF16),
        compiler_params=PARAMS,
        name="source",
    )(in_hbm(acts), in_hbm(partner))
    first = permute(piece, ("x", "zh", "t"), to_plane(0))
    second = permute(piece, ("x", "zh", "t"), to_plane(1))
    chunk = pl.pallas_call(
        chunk_kernel,
        in_specs=[SMEM] + [VMEM] * 2,
        out_specs=VMEM,
        out_shape=shape((CHUNK, WIDTH), BF16),
        compiler_params=PARAMS,
        name="chunk",
    )(half, first, second)
    plane = exchange(jnp.broadcast_to(chunk[None], (16,) + chunk.shape), ("x", "y"))
    other = permute(plane, ("c",), lambda d: {"c": 1 - d["c"]})
    plane = plane.reshape(4, 4, CHUNK, WIDTH)
    other = other.reshape(4, 4, CHUNK, WIDTH)
    tiles = exchange(plane_sums(plane), ("c", "t"))
    mixed, product, cka, *sent = mix(core, place, tiles, hidden, plane, other, scale)
    arrived, later, last = {}, {}, {}
    for name, values in zip("ab", sent):
        arrived[name] = permute(values, ("t",), flip(1))
    kept = weight_parts(place, product, plane, other)
    halves = {}
    for i, name in enumerate("ab"):
        halves[name], moved = add_one(kept, arrived[name], i)
        later[name] = permute(moved, ("t",), flip(2))
    for name in "ab":
        halves[name], moved = add_two(halves[name], later[name])
        last[name] = permute(moved, ("t",), flip(4))
    grad_weight = add_last(halves["a"], last["a"], halves["b"], last["b"])
    grad_hidden = hidden_gradient(place, core, weights, plane, other, mixed)
    return (grad_hidden, grad_weight, cka[0, 0])


def solution(mesh):
    shape = tuple(SIZES[n] for n in NAMES)
    fine = Mesh(mesh.devices.reshape(shape), NAMES)
    spec = P(("x", "zh", "y", "c"), "t")
    return jax.shard_map(
        local, mesh=fine, in_specs=(spec,) * 4, out_specs=(spec, spec, P()), check_vma=False
    )
```

```python
import functools
import itertools

import jax
import jax.numpy as jnp
from jax import lax
from jax.experimental import pallas as pl
from jax.experimental.pallas import tpu as pltpu
from jax.sharding import Mesh, PartitionSpec as P


NAMES = ("x", "zh", "y", "c", "t")
SIZES = {"x": 4, "zh": 2, "y": 4, "c": 2, "t": 8}
BF16 = jnp.bfloat16
F32 = jnp.float32
ROWS = 128
WIDTH = 256
HALF = ROWS // 2
PART = ROWS // 4
PACKED = 2 * PART + PART // 2
PIECE = ROWS + PACKED
CHUNK = 2 * ROWS + PACKED
PARAMS = pltpu.CompilerParams(vmem_limit_bytes=16 << 20)
VMEM = pl.BlockSpec(memory_space=pltpu.VMEM)
SMEM = pl.BlockSpec(memory_space=pltpu.SMEM)
HBM = pl.BlockSpec(memory_space=pltpu.HBM)


def permutation(names, target):
    pairs = []
    for place in itertools.product(*[range(SIZES[n]) for n in names]):
        goal = target(dict(zip(names, place)))
        source, dest = 0, 0
        for name, coordinate in zip(names, place):
            source = source * SIZES[name] + coordinate
            dest = dest * SIZES[name] + goal[name]
        pairs.append((source, dest))
    return pairs


def permute(values, names, target):
    return lax.ppermute(values, names, permutation(names, target))


def exchange(values, names):
    return lax.all_to_all(values, names, split_axis=0, concat_axis=0)


def to_plane(flip):
    def target(d):
        return {"x": d["t"] // 2, "zh": (d["t"] + flip) % 2, "t": 2 * d["x"] + d["zh"]}

    return target


def gram(values):
    return lax.dot_general(values, values, (((1,), (1,)), ((), ())), preferred_element_type=F32)


def center(values):
    floats = values.astype(F32)
    return (floats - jnp.mean(floats, axis=0, keepdims=True)).astype(BF16)


def split(values, parts):
    pieces = []
    for _ in range(parts):
        piece = values.astype(BF16)
        values = values - piece.astype(F32)
        pieces.append(piece)
    return pieces


def lanes(rows):
    return lax.broadcasted_iota(jnp.int32, (rows, ROWS), 1)


def left(rows):
    return lanes(rows) < HALF


def left_of_half(rows):
    return lax.rem(lanes(rows), HALF) < PART


def pack(values):
    top, bottom = values[:HALF], values[HALF:]
    corner = jnp.where(left(PART), pltpu.roll(top[:PART], HALF, 1), top[PART:])
    diagonal = jnp.where(left(HALF), top, bottom)
    inner = jnp.where(left_of_half(PART), diagonal[:PART], diagonal[PART:])
    half = PART // 2
    outer = jnp.where(
        left_of_half(half), pltpu.roll(diagonal[:half], ROWS - PART, 1), diagonal[half:PART]
    )
    return jnp.concatenate([inner, corner, outer], axis=0)


def unpack(packed):
    inner, corner, outer = packed[:PART], packed[PART : 2 * PART], packed[2 * PART :]
    outer = jnp.concatenate([pltpu.roll(outer, PART, 1), outer], axis=0)
    diagonal = jnp.concatenate([jnp.where(left_of_half(PART), inner, outer), inner], axis=0)
    right = jnp.concatenate([pltpu.roll(corner, HALF, 1), corner], axis=0)
    upper = jnp.concatenate([jnp.where(left(HALF), diagonal, right), diagonal], axis=0)
    rows = lax.broadcasted_iota(jnp.int32, (ROWS, ROWS), 0)
    return jnp.where(lax.div(rows, PART) > lax.div(lanes(ROWS), PART), upper.T, upper)


def two_parts(values):
    return jnp.concatenate(split(values, 2), axis=1)


def joined(parts):
    parts = parts.astype(F32)
    return parts[:, :ROWS] + parts[:, ROWS:]


def in_hbm(values):
    return pltpu.with_memory_space_constraint(values, pltpu.HBM)


def fetch(source, target, semaphores, i):
    copy = pltpu.make_async_copy(source, target, semaphores.at[i])
    copy.start()
    return copy


def source_kernel(acts_hbm, partner_hbm, out_ref, acts_ref, partner_ref, semaphores):
    partner = fetch(partner_hbm, partner_ref, semaphores, 0)
    acts = fetch(acts_hbm, acts_ref, semaphores, 1)
    partner.wait()
    out_ref[ROWS:, :] = two_parts(pack(gram(center(partner_ref[...]))))
    acts.wait()
    out_ref[:ROWS, :] = center(acts_ref[...])


def chunk_kernel(flag_ref, first_ref, second_ref, chunk_ref):
    even = flag_ref[0] == 0
    first, second = first_ref[:ROWS, :], second_ref[:ROWS, :]
    chunk_ref[:ROWS, :] = jnp.where(even, first, second)
    chunk_ref[ROWS : 2 * ROWS, :] = jnp.where(even, second, first)
    chunk_ref[2 * ROWS :, :] = two_parts(joined(first_ref[ROWS:, :]) + joined(second_ref[ROWS:, :]))


def minibatch_grams(plane_ref, first):
    rows = [
        jnp.concatenate(
            [plane_ref[t // 2, first + i, pl.ds((t % 2) * ROWS, ROWS), :] for t in range(8)], axis=1
        )
        for i in range(2)
    ]
    pair = gram(jnp.concatenate(rows, axis=0))
    grams = []
    for i in range(2):
        packed = jnp.zeros((PACKED, ROWS), F32)
        for x in range(4):
            packed = packed + joined(plane_ref[x, first + i, pl.ds(2 * ROWS, PACKED), :])
        block = slice(i * ROWS, (i + 1) * ROWS)
        grams.append((pair[block, block], unpack(packed)))
    return grams


def sums_kernel(plane_ref, tiles_ref):
    sums = jnp.zeros((3, ROWS), F32)
    for gram_x, gram_y in minibatch_grams(plane_ref, 0) + minibatch_grams(plane_ref, 2):
        products = (gram_x * gram_x, gram_y * gram_y, gram_x * gram_y)
        sums = sums + jnp.concatenate([jnp.sum(v, axis=0, keepdims=True) for v in products], axis=0)
    tile = jnp.concatenate([sums, jnp.zeros((5, ROWS), F32)], axis=0)
    tiles_ref[...] = jnp.broadcast_to(tile[None], tiles_ref.shape)


def plane_sums(plane):
    return pl.pallas_call(
        sums_kernel,
        in_specs=[VMEM],
        out_specs=VMEM,
        out_shape=jax.ShapeDtypeStruct((16, 8, ROWS), F32),
        compiler_params=PARAMS,
        name="plane_sums",
    )(plane)


def mix_kernel(
    scale, core_ref, place_ref, tiles_ref, own_ref, hidden_hbm, other_hbm,
    mixed_ref, product_ref, cka_ref, upper_ref, lower_ref, hidden_ref, other_ref, semaphores,
):
    other_copy = fetch(other_hbm, other_ref, semaphores, 0)
    hidden_copy = fetch(hidden_hbm, hidden_ref, semaphores, 1)
    sums = jnp.sum(jnp.sum(tiles_ref[...], axis=0), axis=1, keepdims=True)
    sxx, syy, sxy = sums[0:1], sums[1:2], sums[2:3]
    root = jnp.sqrt(sxx * syy)
    ratio = jnp.broadcast_to(sxy / sxx, (1, ROWS))
    coef = jnp.broadcast_to(-2.0 * scale / root, (1, ROWS))
    cka_ref[...] = jnp.broadcast_to(sxy / root, cka_ref.shape)
    core = core_ref[0]

    def mix_pair(ref, base, first):
        for i, (gram_x, gram_y) in enumerate(minibatch_grams(ref, first)):
            mixed_ref[base + first + i] = coef * (gram_y - ratio * gram_x)

    mix_pair(own_ref, 0, 0)
    mix_pair(own_ref, 0, 2)
    other_copy.wait()
    mix_pair(other_ref, 4, 0)
    mix_pair(other_ref, 4, 2)
    hidden_copy.wait()
    for b in range(8):
        place = b % 4 * 2 + (core if b < 4 else 1 - core)
        hidden = hidden_ref[:, pl.ds(pl.multiple_of(place * ROWS, ROWS), ROWS)]
        product = jnp.dot(
            jnp.concatenate([hidden, hidden], axis=1),
            jnp.concatenate(split(mixed_ref[b], 2), axis=0),
            preferred_element_type=F32,
        )
        product_ref[:, b * ROWS : (b + 1) * ROWS] = product.astype(BF16)
    middle = upper_ref.shape[1]
    for k in range(4):
        value = weight_block(place_ref, product_ref, own_ref, other_ref, 4 + k).astype(BF16)
        upper_ref[k] = value[:middle]
        lower_ref[k] = value[middle:]


def mix(core, place, tiles, hidden, plane, other, scale):
    units = hidden.shape[0]
    half = jax.ShapeDtypeStruct((4, units // 2, WIDTH), BF16)
    return pl.pallas_call(
        functools.partial(mix_kernel, scale),
        in_specs=[SMEM] * 2 + [VMEM] * 2 + [HBM] * 2,
        out_specs=[VMEM] * 5,
        out_shape=[
            jax.ShapeDtypeStruct((8, ROWS, ROWS), F32),
            jax.ShapeDtypeStruct(hidden.shape, BF16),
            jax.ShapeDtypeStruct((8, ROWS), F32),
            half,
            half,
        ],
        scratch_shapes=[
            pltpu.VMEM(hidden.shape, BF16),
            pltpu.VMEM(other.shape, BF16),
            pltpu.SemaphoreType.DMA((2,)),
        ],
        compiler_params=PARAMS,
        name="mix",
    )(core, place, tiles, plane, in_hbm(hidden), other)


def column_block(place, k):
    return lax.bitwise_xor(place, (k % 2) * 4 + (k // 2 % 2) * 2 + k // 4)


def token_rows(ref, t):
    start = pl.multiple_of(lax.rem(t, 2) * ROWS, ROWS)
    return ref[lax.div(t, 2), :, pl.ds(start, ROWS), :].reshape(4 * ROWS, WIDTH)


def weight_block(place_ref, product_ref, own_ref, other_ref, k):
    half = 4 * ROWS
    t = column_block(place_ref[0], k)
    value = jnp.dot(product_ref[:, :half], token_rows(own_ref, t), preferred_element_type=F32)
    return value + jnp.dot(
        product_ref[:, half:], token_rows(other_ref, t), preferred_element_type=F32
    )


def weight_kernel(place_ref, product_ref, own_ref, other_ref, out_ref):
    for k in range(4):
        out_ref[k] = weight_block(place_ref, product_ref, own_ref, other_ref, k)


def weight_parts(place, product, plane, other):
    units = product.shape[0]
    return pl.pallas_call(
        weight_kernel,
        in_specs=[SMEM] + [VMEM] * 3,
        out_specs=VMEM,
        out_shape=jax.ShapeDtypeStruct((4, units, WIDTH), F32),
        compiler_params=PARAMS,
        cost_estimate=pl.CostEstimate(
            flops=2 * units * 8 * ROWS * 4 * WIDTH, bytes_accessed=4 << 20, transcendentals=0
        ),
        name="weight_parts",
    )(place, product, plane, other)


def hidden_kernel(
    place_ref, core_ref, near_ref, two_ref, one_ref, three_ref, own_ref, mixed_ref, other_hbm,
    out_ref, other_ref, semaphores,
):
    other_copy = fetch(other_hbm, other_ref, semaphores, 0)
    weights = [ref[i] for ref in (near_ref, two_ref, one_ref, three_ref) for i in range(2)]
    for ref, first in ((own_ref, 0), (other_ref, 4)):
        if first == 4:
            other_copy.wait()
        total = None
        for k in range(8):
            product = lax.dot_general(
                weights[k],
                token_rows(ref, column_block(place_ref[0], k)),
                (((1,), (1,)), ((), ())),
                preferred_element_type=F32,
            )
            total = product if total is None else total + product
        for y in range(4):
            high, low = split(total[:, y * ROWS : (y + 1) * ROWS], 2)
            mixed_high, mixed_low = split(mixed_ref[first + y], 2)
            value = lax.dot_general(
                jnp.concatenate([high, high, low], axis=1),
                jnp.concatenate([mixed_high, mixed_low, mixed_high], axis=1),
                (((1,), (1,)), ((), ())),
                preferred_element_type=F32,
            )
            place = y * 2 + (core_ref[0] if first == 0 else 1 - core_ref[0])
            out_ref[:, pl.ds(pl.multiple_of(place * ROWS, ROWS), ROWS)] = value.astype(BF16)


def hidden_gradient(place, core, weights, plane, other, mixed):
    units = weights[0].shape[1]
    tokens = 8 * ROWS
    return pl.pallas_call(
        hidden_kernel,
        in_specs=[SMEM] * 2 + [VMEM] * 6 + [HBM],
        out_specs=VMEM,
        out_shape=jax.ShapeDtypeStruct((units, tokens), BF16),
        scratch_shapes=[pltpu.VMEM(other.shape, BF16), pltpu.SemaphoreType.DMA((1,))],
        compiler_params=PARAMS,
        cost_estimate=pl.CostEstimate(
            flops=2 * units * tokens * 8 * WIDTH, bytes_accessed=8 << 20, transcendentals=0
        ),
        name="hidden_gradient",
    )(place, core, *weights, plane, mixed, other)


def add_one_kernel(row, kept_ref, arrived_ref, out_ref, moved_ref):
    value = kept_ref[:, row : row + arrived_ref.shape[1]] + arrived_ref[...].astype(F32)
    out_ref[...] = value[:2]
    moved_ref[...] = value[2:].astype(BF16)


def add_one(kept, arrived, half):
    rows = arrived.shape[1]
    return pl.pallas_call(
        functools.partial(add_one_kernel, half * rows),
        in_specs=[VMEM] * 2,
        out_specs=[VMEM] * 2,
        out_shape=[
            jax.ShapeDtypeStruct((2, rows, WIDTH), F32),
            jax.ShapeDtypeStruct((2, rows, WIDTH), BF16),
        ],
        compiler_params=PARAMS,
    )(kept, arrived)


def add_two_kernel(kept_ref, arrived_ref, out_ref, moved_ref):
    value = kept_ref[...] + arrived_ref[...].astype(F32)
    out_ref[...] = value[0]
    moved_ref[...] = value[1].astype(BF16)


def add_two(kept, arrived):
    rows = arrived.shape[1]
    return pl.pallas_call(
        add_two_kernel,
        in_specs=[VMEM] * 2,
        out_specs=[VMEM] * 2,
        out_shape=[
            jax.ShapeDtypeStruct((rows, WIDTH), F32),
            jax.ShapeDtypeStruct((rows, WIDTH), BF16),
        ],
        compiler_params=PARAMS,
    )(kept, arrived)


def add_last_kernel(first_ref, one_ref, second_ref, two_ref, out_ref):
    rows = first_ref.shape[0]
    out_ref[:rows] = first_ref[...] + one_ref[...].astype(F32)
    out_ref[rows:] = second_ref[...] + two_ref[...].astype(F32)


def add_last(*values):
    return pl.pallas_call(
        add_last_kernel,
        in_specs=[VMEM] * 4,
        out_specs=VMEM,
        out_shape=jax.ShapeDtypeStruct((2 * values[0].shape[0], WIDTH), F32),
        compiler_params=PARAMS,
        name="add_last",
    )(*values)


def flip(bit):
    return lambda d: {"t": d["t"] ^ bit}


def local(acts, partner, hidden, down_weight):
    scale = float(ROWS * 64 * WIDTH * 8)
    shape = jax.ShapeDtypeStruct
    place = lax.axis_index("t").astype(jnp.int32).reshape(1)
    core = lax.axis_index("c").astype(jnp.int32).reshape(1)
    half = lax.axis_index("zh").astype(jnp.int32).reshape(1)
    near = down_weight[None]
    far = permute(near, ("t",), flip(4))
    near = jnp.concatenate([near, far], axis=0)
    weights = [near]
    for bit in (2, 1, 3):
        weights.append(permute(near, ("t",), flip(bit)))
    piece = pl.pallas_call(
        source_kernel,
        in_specs=[HBM] * 2,
        out_specs=VMEM,
        scratch_shapes=[pltpu.VMEM((ROWS, WIDTH), BF16)] * 2 + [pltpu.SemaphoreType.DMA((2,))],
        out_shape=shape((PIECE, WIDTH), BF16),
        compiler_params=PARAMS,
        name="source",
    )(in_hbm(acts), in_hbm(partner))
    first = permute(piece, ("x", "zh", "t"), to_plane(0))
    second = permute(piece, ("x", "zh", "t"), to_plane(1))
    chunk = pl.pallas_call(
        chunk_kernel,
        in_specs=[SMEM] + [VMEM] * 2,
        out_specs=VMEM,
        out_shape=shape((CHUNK, WIDTH), BF16),
        compiler_params=PARAMS,
        name="chunk",
    )(half, first, second)
    plane = exchange(jnp.broadcast_to(chunk[None], (16,) + chunk.shape), ("x", "y"))
    other = permute(plane, ("c",), lambda d: {"c": 1 - d["c"]})
    plane = plane.reshape(4, 4, CHUNK, WIDTH)
    other = other.reshape(4, 4, CHUNK, WIDTH)
    tiles = exchange(plane_sums(plane), ("c", "t"))
    mixed, product, cka, *sent = mix(core, place, tiles, hidden, plane, other, scale)
    arrived, later, last = {}, {}, {}
    for name, values in zip("ab", sent):
        arrived[name] = permute(values, ("t",), flip(1))
    kept = weight_parts(place, product, plane, other)
    halves = {}
    for i, name in enumerate("ab"):
        halves[name], moved = add_one(kept, arrived[name], i)
        later[name] = permute(moved, ("t",), flip(2))
    for name in "ab":
        halves[name], moved = add_two(halves[name], later[name])
        last[name] = permute(moved, ("t",), flip(4))
    grad_weight = add_last(halves["a"], last["a"], halves["b"], last["b"])
    grad_hidden = hidden_gradient(place, core, weights, plane, other, mixed)
    return (grad_hidden, grad_weight, cka[0, 0])


def solution(mesh):
    shape = tuple(SIZES[n] for n in NAMES)
    fine = Mesh(mesh.devices.reshape(shape), NAMES)
    spec = P(("x", "zh", "y", "c"), "t")
    return jax.shard_map(
        local, mesh=fine, in_specs=(spec,) * 4, out_specs=(spec, spec, P()), check_vma=False
    )
```

```python
import functools
import itertools

import jax
import jax.numpy as jnp
from jax import lax
from jax.experimental import pallas as pl
from jax.experimental.pallas import tpu as pltpu
from jax.sharding import Mesh, PartitionSpec as P


NAMES = ("x", "zh", "y", "c", "t")
SIZES = {"x": 4, "zh": 2, "y": 4, "c": 2, "t": 8}
BF16 = jnp.bfloat16
F32 = jnp.float32
ROWS = 128
WIDTH = 256
HALF = ROWS // 2
PART = ROWS // 4
PACKED = 2 * PART + PART // 2
PIECE = ROWS + PACKED
CHUNK = 2 * ROWS + PACKED
PARAMS = pltpu.CompilerParams(vmem_limit_bytes=16 << 20)
VMEM = pl.BlockSpec(memory_space=pltpu.VMEM)
SMEM = pl.BlockSpec(memory_space=pltpu.SMEM)
HBM = pl.BlockSpec(memory_space=pltpu.HBM)


def permutation(names, target):
    pairs = []
    for place in itertools.product(*[range(SIZES[n]) for n in names]):
        goal = target(dict(zip(names, place)))
        source, dest = 0, 0
        for name, coordinate in zip(names, place):
            source = source * SIZES[name] + coordinate
            dest = dest * SIZES[name] + goal[name]
        pairs.append((source, dest))
    return pairs


def permute(values, names, target):
    return lax.ppermute(values, names, permutation(names, target))


def exchange(values, names):
    return lax.all_to_all(values, names, split_axis=0, concat_axis=0)


def to_plane(flip):
    def target(d):
        return {"x": d["t"] // 2, "zh": (d["t"] + flip) % 2, "t": 2 * d["x"] + d["zh"]}

    return target


def gram(values):
    return lax.dot_general(values, values, (((1,), (1,)), ((), ())), preferred_element_type=F32)


def center(values):
    floats = values.astype(F32)
    return (floats - jnp.mean(floats, axis=0, keepdims=True)).astype(BF16)


def split(values, parts):
    pieces = []
    for _ in range(parts):
        piece = values.astype(BF16)
        values = values - piece.astype(F32)
        pieces.append(piece)
    return pieces


def lanes(rows):
    return lax.broadcasted_iota(jnp.int32, (rows, ROWS), 1)


def left(rows):
    return lanes(rows) < HALF


def left_of_half(rows):
    return lax.rem(lanes(rows), HALF) < PART


def pack(values):
    top, bottom = values[:HALF], values[HALF:]
    corner = jnp.where(left(PART), pltpu.roll(top[:PART], HALF, 1), top[PART:])
    diagonal = jnp.where(left(HALF), top, bottom)
    inner = jnp.where(left_of_half(PART), diagonal[:PART], diagonal[PART:])
    half = PART // 2
    outer = jnp.where(
        left_of_half(half), pltpu.roll(diagonal[:half], ROWS - PART, 1), diagonal[half:PART]
    )
    return jnp.concatenate([inner, corner, outer], axis=0)


def unpack(packed):
    inner, corner, outer = packed[:PART], packed[PART : 2 * PART], packed[2 * PART :]
    outer = jnp.concatenate([pltpu.roll(outer, PART, 1), outer], axis=0)
    diagonal = jnp.concatenate([jnp.where(left_of_half(PART), inner, outer), inner], axis=0)
    right = jnp.concatenate([pltpu.roll(corner, HALF, 1), corner], axis=0)
    upper = jnp.concatenate([jnp.where(left(HALF), diagonal, right), diagonal], axis=0)
    rows = lax.broadcasted_iota(jnp.int32, (ROWS, ROWS), 0)
    return jnp.where(lax.div(rows, PART) > lax.div(lanes(ROWS), PART), upper.T, upper)


def two_parts(values):
    return jnp.concatenate(split(values, 2), axis=1)


def joined(parts):
    parts = parts.astype(F32)
    return parts[:, :ROWS] + parts[:, ROWS:]


def in_hbm(values):
    return pltpu.with_memory_space_constraint(values, pltpu.HBM)


def fetch(source, target, semaphores, i):
    copy = pltpu.make_async_copy(source, target, semaphores.at[i])
    copy.start()
    return copy


def source_kernel(acts_hbm, partner_hbm, out_ref, acts_ref, partner_ref, semaphores):
    partner = fetch(partner_hbm, partner_ref, semaphores, 0)
    acts = fetch(acts_hbm, acts_ref, semaphores, 1)
    partner.wait()
    out_ref[ROWS:, :] = two_parts(pack(gram(center(partner_ref[...]))))
    acts.wait()
    out_ref[:ROWS, :] = center(acts_ref[...])


def chunk_kernel(flag_ref, first_ref, second_ref, chunk_ref):
    even = flag_ref[0] == 0
    first, second = first_ref[:ROWS, :], second_ref[:ROWS, :]
    chunk_ref[:ROWS, :] = jnp.where(even, first, second)
    chunk_ref[ROWS : 2 * ROWS, :] = jnp.where(even, second, first)
    chunk_ref[2 * ROWS :, :] = two_parts(joined(first_ref[ROWS:, :]) + joined(second_ref[ROWS:, :]))


def minibatch_grams(plane_ref, first):
    rows = [
        jnp.concatenate(
            [plane_ref[t // 2, first + i, pl.ds((t % 2) * ROWS, ROWS), :] for t in range(8)], axis=1
        )
        for i in range(2)
    ]
    pair = gram(jnp.concatenate(rows, axis=0))
    grams = []
    for i in range(2):
        packed = jnp.zeros((PACKED, ROWS), F32)
        for x in range(4):
            packed = packed + joined(plane_ref[x, first + i, pl.ds(2 * ROWS, PACKED), :])
        block = slice(i * ROWS, (i + 1) * ROWS)
        grams.append((pair[block, block], unpack(packed)))
    return grams


def sums_kernel(plane_ref, tiles_ref):
    sums = jnp.zeros((3, ROWS), F32)
    for gram_x, gram_y in minibatch_grams(plane_ref, 0) + minibatch_grams(plane_ref, 2):
        products = (gram_x * gram_x, gram_y * gram_y, gram_x * gram_y)
        sums = sums + jnp.concatenate([jnp.sum(v, axis=0, keepdims=True) for v in products], axis=0)
    tile = jnp.concatenate([sums, jnp.zeros((5, ROWS), F32)], axis=0)
    tiles_ref[...] = jnp.broadcast_to(tile[None], tiles_ref.shape)


def plane_sums(plane):
    return pl.pallas_call(
        sums_kernel,
        in_specs=[VMEM],
        out_specs=VMEM,
        out_shape=jax.ShapeDtypeStruct((16, 8, ROWS), F32),
        compiler_params=PARAMS,
        name="plane_sums",
    )(plane)


def mix_kernel(
    scale, core_ref, place_ref, tiles_ref, own_ref, hidden_hbm, other_hbm,
    mixed_ref, product_ref, cka_ref, upper_ref, lower_ref, hidden_ref, other_ref, semaphores,
):
    other_copy = fetch(other_hbm, other_ref, semaphores, 0)
    hidden_copy = fetch(hidden_hbm, hidden_ref, semaphores, 1)
    sums = jnp.sum(jnp.sum(tiles_ref[...], axis=0), axis=1, keepdims=True)
    sxx, syy, sxy = sums[0:1], sums[1:2], sums[2:3]
    root = jnp.sqrt(sxx * syy)
    ratio = jnp.broadcast_to(sxy / sxx, (1, ROWS))
    coef = jnp.broadcast_to(-2.0 * scale / root, (1, ROWS))
    cka_ref[...] = sxy / root
    core = core_ref[0]

    def mix_pair(ref, base, first):
        for i, (gram_x, gram_y) in enumerate(minibatch_grams(ref, first)):
            mixed_ref[base + first + i] = coef * (gram_y - ratio * gram_x)

    mix_pair(own_ref, 0, 0)
    mix_pair(own_ref, 0, 2)
    other_copy.wait()
    mix_pair(other_ref, 4, 0)
    mix_pair(other_ref, 4, 2)
    hidden_copy.wait()
    for b in range(8):
        place = b % 4 * 2 + (core if b < 4 else 1 - core)
        hidden = hidden_ref[:, pl.ds(pl.multiple_of(place * ROWS, ROWS), ROWS)]
        product = jnp.dot(
            jnp.concatenate([hidden, hidden], axis=1),
            jnp.concatenate(split(mixed_ref[b], 2), axis=0),
            preferred_element_type=F32,
        )
        product_ref[:, b * ROWS : (b + 1) * ROWS] = product.astype(BF16)
    middle = upper_ref.shape[1]
    for k in range(4):
        value = weight_block(place_ref, product_ref, own_ref, other_ref, 4 + k).astype(BF16)
        upper_ref[k] = value[:middle]
        lower_ref[k] = value[middle:]


def mix(core, place, tiles, hidden, plane, other, scale):
    units = hidden.shape[0]
    half = jax.ShapeDtypeStruct((4, units // 2, WIDTH), BF16)
    return pl.pallas_call(
        functools.partial(mix_kernel, scale),
        in_specs=[SMEM] * 2 + [VMEM] * 2 + [HBM] * 2,
        out_specs=[VMEM] * 5,
        out_shape=[
            jax.ShapeDtypeStruct((8, ROWS, ROWS), F32),
            jax.ShapeDtypeStruct(hidden.shape, BF16),
            jax.ShapeDtypeStruct((1, 1), F32),
            half,
            half,
        ],
        scratch_shapes=[
            pltpu.VMEM(hidden.shape, BF16),
            pltpu.VMEM(other.shape, BF16),
            pltpu.SemaphoreType.DMA((2,)),
        ],
        compiler_params=PARAMS,
        name="mix",
    )(core, place, tiles, plane, in_hbm(hidden), other)


def column_block(place, k):
    return lax.bitwise_xor(place, (k % 2) * 4 + (k // 2 % 2) * 2 + k // 4)


def token_rows(ref, t):
    start = pl.multiple_of(lax.rem(t, 2) * ROWS, ROWS)
    return ref[lax.div(t, 2), :, pl.ds(start, ROWS), :].reshape(4 * ROWS, WIDTH)


def weight_block(place_ref, product_ref, own_ref, other_ref, k):
    half = 4 * ROWS
    t = column_block(place_ref[0], k)
    value = jnp.dot(product_ref[:, :half], token_rows(own_ref, t), preferred_element_type=F32)
    return value + jnp.dot(
        product_ref[:, half:], token_rows(other_ref, t), preferred_element_type=F32
    )


def weight_kernel(place_ref, product_ref, own_ref, other_ref, out_ref):
    for k in range(4):
        out_ref[k] = weight_block(place_ref, product_ref, own_ref, other_ref, k)


def weight_parts(place, product, plane, other):
    units = product.shape[0]
    return pl.pallas_call(
        weight_kernel,
        in_specs=[SMEM] + [VMEM] * 3,
        out_specs=VMEM,
        out_shape=jax.ShapeDtypeStruct((4, units, WIDTH), F32),
        compiler_params=PARAMS,
        cost_estimate=pl.CostEstimate(
            flops=2 * units * 8 * ROWS * 4 * WIDTH, bytes_accessed=4 << 20, transcendentals=0
        ),
        name="weight_parts",
    )(place, product, plane, other)


def hidden_kernel(
    place_ref, core_ref, near_ref, two_ref, one_ref, three_ref, own_ref, mixed_ref, other_hbm,
    out_ref, other_ref, semaphores,
):
    other_copy = fetch(other_hbm, other_ref, semaphores, 0)
    weights = [ref[i] for ref in (near_ref, two_ref, one_ref, three_ref) for i in range(2)]
    for ref, first in ((own_ref, 0), (other_ref, 4)):
        if first == 4:
            other_copy.wait()
        total = None
        for k in range(8):
            product = lax.dot_general(
                weights[k],
                token_rows(ref, column_block(place_ref[0], k)),
                (((1,), (1,)), ((), ())),
                preferred_element_type=F32,
            )
            total = product if total is None else total + product
        for y in range(4):
            high, low = split(total[:, y * ROWS : (y + 1) * ROWS], 2)
            mixed_high, mixed_low = split(mixed_ref[first + y], 2)
            value = lax.dot_general(
                jnp.concatenate([high, high, low], axis=1),
                jnp.concatenate([mixed_high, mixed_low, mixed_high], axis=1),
                (((1,), (1,)), ((), ())),
                preferred_element_type=F32,
            )
            place = y * 2 + (core_ref[0] if first == 0 else 1 - core_ref[0])
            out_ref[:, pl.ds(pl.multiple_of(place * ROWS, ROWS), ROWS)] = value.astype(BF16)


def hidden_gradient(place, core, weights, plane, other, mixed):
    units = weights[0].shape[1]
    tokens = 8 * ROWS
    return pl.pallas_call(
        hidden_kernel,
        in_specs=[SMEM] * 2 + [VMEM] * 6 + [HBM],
        out_specs=VMEM,
        out_shape=jax.ShapeDtypeStruct((units, tokens), BF16),
        scratch_shapes=[pltpu.VMEM(other.shape, BF16), pltpu.SemaphoreType.DMA((1,))],
        compiler_params=PARAMS,
        cost_estimate=pl.CostEstimate(
            flops=2 * units * tokens * 8 * WIDTH, bytes_accessed=8 << 20, transcendentals=0
        ),
        name="hidden_gradient",
    )(place, core, *weights, plane, mixed, other)


def add_one_kernel(row, kept_ref, arrived_ref, out_ref, moved_ref):
    value = kept_ref[:, row : row + arrived_ref.shape[1]] + arrived_ref[...].astype(F32)
    out_ref[...] = value[:2]
    moved_ref[...] = value[2:].astype(BF16)


def add_one(kept, arrived, half):
    rows = arrived.shape[1]
    return pl.pallas_call(
        functools.partial(add_one_kernel, half * rows),
        in_specs=[VMEM] * 2,
        out_specs=[VMEM] * 2,
        out_shape=[
            jax.ShapeDtypeStruct((2, rows, WIDTH), F32),
            jax.ShapeDtypeStruct((2, rows, WIDTH), BF16),
        ],
        compiler_params=PARAMS,
    )(kept, arrived)


def add_two_kernel(kept_ref, arrived_ref, out_ref, moved_ref):
    value = kept_ref[...] + arrived_ref[...].astype(F32)
    out_ref[...] = value[0]
    moved_ref[...] = value[1].astype(BF16)


def add_two(kept, arrived):
    rows = arrived.shape[1]
    return pl.pallas_call(
        add_two_kernel,
        in_specs=[VMEM] * 2,
        out_specs=[VMEM] * 2,
        out_shape=[
            jax.ShapeDtypeStruct((rows, WIDTH), F32),
            jax.ShapeDtypeStruct((rows, WIDTH), BF16),
        ],
        compiler_params=PARAMS,
    )(kept, arrived)


def add_last_kernel(first_ref, one_ref, second_ref, two_ref, out_ref):
    rows = first_ref.shape[0]
    out_ref[:rows] = first_ref[...] + one_ref[...].astype(F32)
    out_ref[rows:] = second_ref[...] + two_ref[...].astype(F32)


def add_last(*values):
    return pl.pallas_call(
        add_last_kernel,
        in_specs=[VMEM] * 4,
        out_specs=VMEM,
        out_shape=jax.ShapeDtypeStruct((2 * values[0].shape[0], WIDTH), F32),
        compiler_params=PARAMS,
        name="add_last",
    )(*values)


def flip(bit):
    return lambda d: {"t": d["t"] ^ bit}


def local(acts, partner, hidden, down_weight):
    scale = float(ROWS * 64 * WIDTH * 8)
    shape = jax.ShapeDtypeStruct
    place = lax.axis_index("t").astype(jnp.int32).reshape(1)
    core = lax.axis_index("c").astype(jnp.int32).reshape(1)
    half = lax.axis_index("zh").astype(jnp.int32).reshape(1)
    near = down_weight[None]
    far = permute(near, ("t",), flip(4))
    near = jnp.concatenate([near, far], axis=0)
    weights = [near]
    for bit in (2, 1, 3):
        weights.append(permute(near, ("t",), flip(bit)))
    piece = pl.pallas_call(
        source_kernel,
        in_specs=[HBM] * 2,
        out_specs=VMEM,
        scratch_shapes=[pltpu.VMEM((ROWS, WIDTH), BF16)] * 2 + [pltpu.SemaphoreType.DMA((2,))],
        out_shape=shape((PIECE, WIDTH), BF16),
        compiler_params=PARAMS,
        name="source",
    )(in_hbm(acts), in_hbm(partner))
    first = permute(piece, ("x", "zh", "t"), to_plane(0))
    second = permute(piece, ("x", "zh", "t"), to_plane(1))
    chunk = pl.pallas_call(
        chunk_kernel,
        in_specs=[SMEM] + [VMEM] * 2,
        out_specs=VMEM,
        out_shape=shape((CHUNK, WIDTH), BF16),
        compiler_params=PARAMS,
        name="chunk",
    )(half, first, second)
    plane = exchange(jnp.broadcast_to(chunk[None], (16,) + chunk.shape), ("x", "y"))
    other = permute(plane, ("c",), lambda d: {"c": 1 - d["c"]})
    plane = plane.reshape(4, 4, CHUNK, WIDTH)
    other = other.reshape(4, 4, CHUNK, WIDTH)
    tiles = exchange(plane_sums(plane), ("c", "t"))
    mixed, product, cka, *sent = mix(core, place, tiles, hidden, plane, other, scale)
    arrived, later, last = {}, {}, {}
    for name, values in zip("ab", sent):
        arrived[name] = permute(values, ("t",), flip(1))
    kept = weight_parts(place, product, plane, other)
    halves = {}
    for i, name in enumerate("ab"):
        halves[name], moved = add_one(kept, arrived[name], i)
        later[name] = permute(moved, ("t",), flip(2))
    for name in "ab":
        halves[name], moved = add_two(halves[name], later[name])
        last[name] = permute(moved, ("t",), flip(4))
    grad_weight = add_last(halves["a"], last["a"], halves["b"], last["b"])
    grad_hidden = hidden_gradient(place, core, weights, plane, other, mixed)
    return (grad_hidden, grad_weight, cka.reshape(()))


def solution(mesh):
    shape = tuple(SIZES[n] for n in NAMES)
    fine = Mesh(mesh.devices.reshape(shape), NAMES)
    spec = P(("x", "zh", "y", "c"), "t")
    return jax.shard_map(
        local, mesh=fine, in_specs=(spec,) * 4, out_specs=(spec, spec, P()), check_vma=False
    )
```

```python
import functools
import itertools

import jax
import jax.numpy as jnp
from jax import lax
from jax.experimental import pallas as pl
from jax.experimental.pallas import tpu as pltpu
from jax.sharding import Mesh, PartitionSpec as P


NAMES = ("x", "zh", "y", "c", "t")
SIZES = {"x": 4, "zh": 2, "y": 4, "c": 2, "t": 8}
BF16 = jnp.bfloat16
F32 = jnp.float32
ROWS = 128
WIDTH = 256
HALF = ROWS // 2
PART = ROWS // 4
PACKED = 2 * PART + PART // 2
PIECE = ROWS + PACKED
CHUNK = 2 * ROWS + PACKED
PARAMS = pltpu.CompilerParams(vmem_limit_bytes=16 << 20)
VMEM = pl.BlockSpec(memory_space=pltpu.VMEM)
SMEM = pl.BlockSpec(memory_space=pltpu.SMEM)
HBM = pl.BlockSpec(memory_space=pltpu.HBM)


def permutation(names, target):
    pairs = []
    for place in itertools.product(*[range(SIZES[n]) for n in names]):
        goal = target(dict(zip(names, place)))
        source, dest = 0, 0
        for name, coordinate in zip(names, place):
            source = source * SIZES[name] + coordinate
            dest = dest * SIZES[name] + goal[name]
        pairs.append((source, dest))
    return pairs


def permute(values, names, target):
    return lax.ppermute(values, names, permutation(names, target))


def exchange(values, names):
    return lax.all_to_all(values, names, split_axis=0, concat_axis=0)


def to_plane(flip):
    def target(d):
        return {"x": d["t"] // 2, "zh": (d["t"] + flip) % 2, "t": 2 * d["x"] + d["zh"]}

    return target


def gram(values):
    return lax.dot_general(values, values, (((1,), (1,)), ((), ())), preferred_element_type=F32)


def center(values):
    floats = values.astype(F32)
    return (floats - jnp.mean(floats, axis=0, keepdims=True)).astype(BF16)


def split(values, parts):
    pieces = []
    for _ in range(parts):
        piece = values.astype(BF16)
        values = values - piece.astype(F32)
        pieces.append(piece)
    return pieces


def lanes(rows):
    return lax.broadcasted_iota(jnp.int32, (rows, ROWS), 1)


def left(rows):
    return lanes(rows) < HALF


def left_of_half(rows):
    return lax.rem(lanes(rows), HALF) < PART


def pack(values):
    top, bottom = values[:HALF], values[HALF:]
    corner = jnp.where(left(PART), pltpu.roll(top[:PART], HALF, 1), top[PART:])
    diagonal = jnp.where(left(HALF), top, bottom)
    inner = jnp.where(left_of_half(PART), diagonal[:PART], diagonal[PART:])
    half = PART // 2
    outer = jnp.where(
        left_of_half(half), pltpu.roll(diagonal[:half], ROWS - PART, 1), diagonal[half:PART]
    )
    return jnp.concatenate([inner, corner, outer], axis=0)


def unpack(packed):
    inner, corner, outer = packed[:PART], packed[PART : 2 * PART], packed[2 * PART :]
    outer = jnp.concatenate([pltpu.roll(outer, PART, 1), outer], axis=0)
    diagonal = jnp.concatenate([jnp.where(left_of_half(PART), inner, outer), inner], axis=0)
    right = jnp.concatenate([pltpu.roll(corner, HALF, 1), corner], axis=0)
    upper = jnp.concatenate([jnp.where(left(HALF), diagonal, right), diagonal], axis=0)
    rows = lax.broadcasted_iota(jnp.int32, (ROWS, ROWS), 0)
    return jnp.where(lax.div(rows, PART) > lax.div(lanes(ROWS), PART), upper.T, upper)


def two_parts(values):
    return jnp.concatenate(split(values, 2), axis=1)


def joined(parts):
    parts = parts.astype(F32)
    return parts[:, :ROWS] + parts[:, ROWS:]


def in_hbm(values):
    return pltpu.with_memory_space_constraint(values, pltpu.HBM)


def fetch(source, target, semaphores, i):
    copy = pltpu.make_async_copy(source, target, semaphores.at[i])
    copy.start()
    return copy


def source_kernel(acts_hbm, partner_hbm, out_ref, acts_ref, partner_ref, semaphores):
    partner = fetch(partner_hbm, partner_ref, semaphores, 0)
    acts = fetch(acts_hbm, acts_ref, semaphores, 1)
    partner.wait()
    out_ref[ROWS:, :] = two_parts(pack(gram(center(partner_ref[...]))))
    acts.wait()
    out_ref[:ROWS, :] = center(acts_ref[...])


def chunk_kernel(flag_ref, first_ref, second_ref, chunk_ref):
    even = flag_ref[0] == 0
    first, second = first_ref[:ROWS, :], second_ref[:ROWS, :]
    chunk_ref[:ROWS, :] = jnp.where(even, first, second)
    chunk_ref[ROWS : 2 * ROWS, :] = jnp.where(even, second, first)
    chunk_ref[2 * ROWS :, :] = two_parts(joined(first_ref[ROWS:, :]) + joined(second_ref[ROWS:, :]))


def minibatch_grams(plane_ref, first):
    rows = [
        jnp.concatenate(
            [plane_ref[t // 2, first + i, pl.ds((t % 2) * ROWS, ROWS), :] for t in range(8)], axis=1
        )
        for i in range(2)
    ]
    pair = gram(jnp.concatenate(rows, axis=0))
    grams = []
    for i in range(2):
        packed = jnp.zeros((PACKED, ROWS), F32)
        for x in range(4):
            packed = packed + joined(plane_ref[x, first + i, pl.ds(2 * ROWS, PACKED), :])
        block = slice(i * ROWS, (i + 1) * ROWS)
        grams.append((pair[block, block], unpack(packed)))
    return grams


def sums_kernel(plane_ref, tiles_ref):
    sums = jnp.zeros((3, ROWS), F32)
    for gram_x, gram_y in minibatch_grams(plane_ref, 0) + minibatch_grams(plane_ref, 2):
        products = (gram_x * gram_x, gram_y * gram_y, gram_x * gram_y)
        sums = sums + jnp.concatenate([jnp.sum(v, axis=0, keepdims=True) for v in products], axis=0)
    tile = jnp.concatenate([sums, jnp.zeros((5, ROWS), F32)], axis=0)
    tiles_ref[...] = jnp.broadcast_to(tile[None], tiles_ref.shape)


def plane_sums(plane):
    return pl.pallas_call(
        sums_kernel,
        in_specs=[VMEM],
        out_specs=VMEM,
        out_shape=jax.ShapeDtypeStruct((16, 8, ROWS), F32),
        compiler_params=PARAMS,
        name="plane_sums",
    )(plane)


def mix_rows(core, mixed_ref, hidden_ref, product_ref):
    for b in range(8):
        place = b % 4 * 2 + (core if b < 4 else 1 - core)
        hidden = hidden_ref[:, pl.ds(pl.multiple_of(place * ROWS, ROWS), ROWS)]
        product = jnp.dot(
            jnp.concatenate([hidden, hidden], axis=1),
            jnp.concatenate(split(mixed_ref[b], 2), axis=0),
            preferred_element_type=F32,
        )
        product_ref[:, b * ROWS : (b + 1) * ROWS] = product.astype(BF16)


def mix_kernel(
    scale, core_ref, place_ref, tiles_ref, own_ref, hidden_hbm, other_hbm,
    mixed_ref, product_ref, cka_ref, upper_ref, lower_ref, hidden_ref, other_ref, semaphores,
):
    pairs = [
        fetch(other_hbm.at[:, pl.ds(y, 2)], other_ref.at[:, pl.ds(y, 2)], semaphores, y // 2)
        for y in (0, 2)
    ]
    hidden_copy = fetch(hidden_hbm, hidden_ref, semaphores, 2)
    sums = jnp.sum(jnp.sum(tiles_ref[...], axis=0), axis=1, keepdims=True)
    sxx, syy, sxy = sums[0:1], sums[1:2], sums[2:3]
    root = jnp.sqrt(sxx * syy)
    ratio = jnp.broadcast_to(sxy / sxx, (1, ROWS))
    coef = jnp.broadcast_to(-2.0 * scale / root, (1, ROWS))
    cka_ref[...] = sxy / root

    def mix_pair(ref, base, first):
        for i, (gram_x, gram_y) in enumerate(minibatch_grams(ref, first)):
            mixed_ref[base + first + i] = coef * (gram_y - ratio * gram_x)

    mix_pair(own_ref, 0, 0)
    mix_pair(own_ref, 0, 2)
    for pair, y in zip(pairs, (0, 2)):
        pair.wait()
        mix_pair(other_ref, 4, y)
    hidden_copy.wait()
    mix_rows(core_ref[0], mixed_ref, hidden_ref, product_ref)
    middle = upper_ref.shape[1]
    for k in range(4):
        value = weight_block(place_ref, product_ref, own_ref, other_ref, 4 + k).astype(BF16)
        upper_ref[k] = value[:middle]
        lower_ref[k] = value[middle:]


def mix(core, place, tiles, hidden, plane, other, scale):
    units = hidden.shape[0]
    half = jax.ShapeDtypeStruct((4, units // 2, WIDTH), BF16)
    return pl.pallas_call(
        functools.partial(mix_kernel, scale),
        in_specs=[SMEM] * 2 + [VMEM] * 2 + [HBM] * 2,
        out_specs=[VMEM] * 5,
        out_shape=[
            jax.ShapeDtypeStruct((8, ROWS, ROWS), F32),
            jax.ShapeDtypeStruct(hidden.shape, BF16),
            jax.ShapeDtypeStruct((1, 1), F32),
            half,
            half,
        ],
        scratch_shapes=[
            pltpu.VMEM(hidden.shape, BF16),
            pltpu.VMEM(other.shape, BF16),
            pltpu.SemaphoreType.DMA((3,)),
        ],
        compiler_params=PARAMS,
        name="mix",
    )(core, place, tiles, plane, in_hbm(hidden), other)


def column_block(place, k):
    return lax.bitwise_xor(place, (k % 2) * 4 + (k // 2 % 2) * 2 + k // 4)


def token_rows(ref, t):
    start = pl.multiple_of(lax.rem(t, 2) * ROWS, ROWS)
    return ref[lax.div(t, 2), :, pl.ds(start, ROWS), :].reshape(4 * ROWS, WIDTH)


def weight_block(place_ref, product_ref, own_ref, other_ref, k):
    half = 4 * ROWS
    t = column_block(place_ref[0], k)
    value = jnp.dot(product_ref[:, :half], token_rows(own_ref, t), preferred_element_type=F32)
    return value + jnp.dot(
        product_ref[:, half:], token_rows(other_ref, t), preferred_element_type=F32
    )


def weight_kernel(place_ref, product_ref, own_ref, other_hbm, out_ref, other_ref, semaphores):
    other_copy = fetch(other_hbm, other_ref, semaphores, 0)
    half = 4 * ROWS
    for k in range(4):
        t = column_block(place_ref[0], k)
        out_ref[k] = jnp.dot(
            product_ref[:, :half], token_rows(own_ref, t), preferred_element_type=F32
        )
    other_copy.wait()
    for k in range(4):
        t = column_block(place_ref[0], k)
        out_ref[k] += jnp.dot(
            product_ref[:, half:], token_rows(other_ref, t), preferred_element_type=F32
        )


def weight_parts(place, product, plane, other):
    units = product.shape[0]
    return pl.pallas_call(
        weight_kernel,
        in_specs=[SMEM] + [VMEM] * 2 + [HBM],
        out_specs=VMEM,
        out_shape=jax.ShapeDtypeStruct((4, units, WIDTH), F32),
        scratch_shapes=[pltpu.VMEM(other.shape, BF16), pltpu.SemaphoreType.DMA((1,))],
        compiler_params=PARAMS,
        cost_estimate=pl.CostEstimate(
            flops=2 * units * 8 * ROWS * 4 * WIDTH, bytes_accessed=4 << 20, transcendentals=0
        ),
        name="weight_parts",
    )(place, product, plane, other)


def hidden_kernel(
    place_ref, core_ref, near_ref, two_ref, one_ref, three_ref, own_ref, mixed_ref, other_hbm,
    out_ref, other_ref, semaphores,
):
    other_copy = fetch(other_hbm, other_ref, semaphores, 0)
    weights = [ref[i] for ref in (near_ref, two_ref, one_ref, three_ref) for i in range(2)]
    for ref, first in ((own_ref, 0), (other_ref, 4)):
        if first == 4:
            other_copy.wait()
        total = None
        for k in range(8):
            product = lax.dot_general(
                weights[k],
                token_rows(ref, column_block(place_ref[0], k)),
                (((1,), (1,)), ((), ())),
                preferred_element_type=F32,
            )
            total = product if total is None else total + product
        for y in range(4):
            high, low = split(total[:, y * ROWS : (y + 1) * ROWS], 2)
            mixed_high, mixed_low = split(mixed_ref[first + y], 2)
            value = lax.dot_general(
                jnp.concatenate([high, high, low], axis=1),
                jnp.concatenate([mixed_high, mixed_low, mixed_high], axis=1),
                (((1,), (1,)), ((), ())),
                preferred_element_type=F32,
            )
            place = y * 2 + (core_ref[0] if first == 0 else 1 - core_ref[0])
            out_ref[:, pl.ds(pl.multiple_of(place * ROWS, ROWS), ROWS)] = value.astype(BF16)


def hidden_gradient(place, core, weights, plane, other, mixed):
    units = weights[0].shape[1]
    tokens = 8 * ROWS
    return pl.pallas_call(
        hidden_kernel,
        in_specs=[SMEM] * 2 + [VMEM] * 6 + [HBM],
        out_specs=VMEM,
        out_shape=jax.ShapeDtypeStruct((units, tokens), BF16),
        scratch_shapes=[pltpu.VMEM(other.shape, BF16), pltpu.SemaphoreType.DMA((1,))],
        compiler_params=PARAMS,
        cost_estimate=pl.CostEstimate(
            flops=2 * units * tokens * 8 * WIDTH, bytes_accessed=8 << 20, transcendentals=0
        ),
        name="hidden_gradient",
    )(place, core, *weights, plane, mixed, other)


def add_one_kernel(row, kept_ref, arrived_ref, out_ref, moved_ref):
    value = kept_ref[:, row : row + arrived_ref.shape[1]] + arrived_ref[...].astype(F32)
    out_ref[...] = value[:2]
    moved_ref[...] = value[2:].astype(BF16)


def add_one(kept, arrived, half):
    rows = arrived.shape[1]
    return pl.pallas_call(
        functools.partial(add_one_kernel, half * rows),
        in_specs=[VMEM] * 2,
        out_specs=[VMEM] * 2,
        out_shape=[
            jax.ShapeDtypeStruct((2, rows, WIDTH), F32),
            jax.ShapeDtypeStruct((2, rows, WIDTH), BF16),
        ],
        compiler_params=PARAMS,
    )(kept, arrived)


def add_two_kernel(kept_ref, arrived_ref, out_ref, moved_ref):
    value = kept_ref[...] + arrived_ref[...].astype(F32)
    out_ref[...] = value[0]
    moved_ref[...] = value[1].astype(BF16)


def add_two(kept, arrived):
    rows = arrived.shape[1]
    return pl.pallas_call(
        add_two_kernel,
        in_specs=[VMEM] * 2,
        out_specs=[VMEM] * 2,
        out_shape=[
            jax.ShapeDtypeStruct((rows, WIDTH), F32),
            jax.ShapeDtypeStruct((rows, WIDTH), BF16),
        ],
        compiler_params=PARAMS,
    )(kept, arrived)


def add_last_kernel(first_ref, one_ref, second_ref, two_ref, out_ref):
    rows = first_ref.shape[0]
    out_ref[:rows] = first_ref[...] + one_ref[...].astype(F32)
    out_ref[rows:] = second_ref[...] + two_ref[...].astype(F32)


def add_last(*values):
    return pl.pallas_call(
        add_last_kernel,
        in_specs=[VMEM] * 4,
        out_specs=VMEM,
        out_shape=jax.ShapeDtypeStruct((2 * values[0].shape[0], WIDTH), F32),
        compiler_params=PARAMS,
        name="add_last",
    )(*values)


def flip(bit):
    return lambda d: {"t": d["t"] ^ bit}


def local(acts, partner, hidden, down_weight):
    scale = float(ROWS * 64 * WIDTH * 8)
    shape = jax.ShapeDtypeStruct
    place = lax.axis_index("t").astype(jnp.int32).reshape(1)
    core = lax.axis_index("c").astype(jnp.int32).reshape(1)
    half = lax.axis_index("zh").astype(jnp.int32).reshape(1)
    near = down_weight[None]
    far = permute(near, ("t",), flip(4))
    near = jnp.concatenate([near, far], axis=0)
    weights = [near]
    for bit in (2, 1, 3):
        weights.append(permute(near, ("t",), flip(bit)))
    piece = pl.pallas_call(
        source_kernel,
        in_specs=[HBM] * 2,
        out_specs=VMEM,
        scratch_shapes=[pltpu.VMEM((ROWS, WIDTH), BF16)] * 2 + [pltpu.SemaphoreType.DMA((2,))],
        out_shape=shape((PIECE, WIDTH), BF16),
        compiler_params=PARAMS,
        name="source",
    )(in_hbm(acts), in_hbm(partner))
    first = permute(piece, ("x", "zh", "t"), to_plane(0))
    second = permute(piece, ("x", "zh", "t"), to_plane(1))
    chunk = pl.pallas_call(
        chunk_kernel,
        in_specs=[SMEM] + [VMEM] * 2,
        out_specs=VMEM,
        out_shape=shape((CHUNK, WIDTH), BF16),
        compiler_params=PARAMS,
        name="chunk",
    )(half, first, second)
    plane = exchange(jnp.broadcast_to(chunk[None], (16,) + chunk.shape), ("x", "y"))
    other = permute(plane, ("c",), lambda d: {"c": 1 - d["c"]})
    plane = plane.reshape(4, 4, CHUNK, WIDTH)
    other = other.reshape(4, 4, CHUNK, WIDTH)
    tiles = exchange(plane_sums(plane), ("c", "t"))
    mixed, product, cka, *sent = mix(core, place, tiles, hidden, plane, other, scale)
    arrived, later, last = {}, {}, {}
    for name, values in zip("ab", sent):
        arrived[name] = permute(values, ("t",), flip(1))
    kept = weight_parts(place, product, plane, other)
    halves = {}
    for i, name in enumerate("ab"):
        halves[name], moved = add_one(kept, arrived[name], i)
        later[name] = permute(moved, ("t",), flip(2))
    for name in "ab":
        halves[name], moved = add_two(halves[name], later[name])
        last[name] = permute(moved, ("t",), flip(4))
    grad_weight = add_last(halves["a"], last["a"], halves["b"], last["b"])
    grad_hidden = hidden_gradient(place, core, weights, plane, other, mixed)
    return (grad_hidden, grad_weight, cka.reshape(()))


def solution(mesh):
    shape = tuple(SIZES[n] for n in NAMES)
    fine = Mesh(mesh.devices.reshape(shape), NAMES)
    spec = P(("x", "zh", "y", "c"), "t")
    return jax.shard_map(
        local, mesh=fine, in_specs=(spec,) * 4, out_specs=(spec, spec, P()), check_vma=False
    )
```
